512 devices in a mesh: tor: 8 (over z_lo, x), pol: 64 (over y, z_hi, core).
Axes of the slice: x: 4, y: 8, z: 8 (z_hi: 4, z_lo: 2; z = z_hi * 2 + z_lo), core: 2. Of those that a mesh axis runs over, the one named last changes fastest.
Arguments:
- plasma_state: float32 [6, 8, 512, 256], P(None, 'tor', 'pol'), may hold values from -3 to 3
- right_side: float32 [6, 8, 512, 256], P(None, 'tor', 'pol'), may hold values from -12 to 12
- resistivity: float32 [8, 512, 256], P('tor', 'pol'), may hold values from 0.05 to 0.6
- jacobi_blocks: float32 [6, 6, 8, 512, 256], P(None, None, 'tor', 'pol'), may hold values from -0.6 to 1.6, as said below
Outputs:
- update: float32 [6, 8, 512, 256], P(None, 'tor', 'pol')
- estimates: float32 [3], replicated
The draws below stay inside these ranges and needn't reach their ends.
Inputs may be any that keep to these rules, and one draw needn't show every extreme that they name: `jacobi_blocks`: each block's diagonal entries lie in 0.4 to 1.6.
All inputs are finite; a program needn't handle non-finite values.
Results may differ from the reference program's by a relative error of at most 0.006.
Values may be sent and summed in bfloat16 or wider, within the bound.
A program may use at most 64 MiB of HBM per device.

```python
import math
import jax
import jax.numpy as jnp
from jax import lax

DEPTH = 256
ITERS = 3
PLANES = 8
ROWS = 512


def draw_right_side(key, part):
    shape = (6, PLANES, ROWS, DEPTH)
    noise_key = jax.random.fold_in(key, 11)
    plane_pos = lax.broadcasted_iota(jnp.float32, shape, 1)
    row_pos = lax.broadcasted_iota(jnp.float32, shape, 2)
    envelope = 1.0 + plane_pos / max(PLANES - 1, 1) + row_pos / max(ROWS - 1, 1)
    noise = jnp.clip(jax.random.normal(noise_key, shape, jnp.float32), -4.0, 4.0)
    return noise * envelope


def draw_jacobi_blocks(key, part):
    shape = (6, 6, PLANES, ROWS, DEPTH)
    diag_key = jax.random.fold_in(key, 21)
    off_key = jax.random.fold_in(key, 22)
    on_diagonal = lax.broadcasted_iota(jnp.int32, shape, 0) == lax.broadcasted_iota(jnp.int32, shape, 1)
    diagonal = jax.random.uniform(diag_key, shape, jnp.float32, 0.6, 1.4)
    coupling = 0.12 * jnp.clip(jax.random.normal(off_key, shape, jnp.float32), -5.0, 5.0)
    return jnp.where(on_diagonal, diagonal, coupling)


def steps_of(stream_key, dims, shards, smallest, top_value):
    def one(position, blocks):
        heights = jax.random.uniform(jax.random.fold_in(jax.random.fold_in(stream_key, 6), position), (blocks,), jnp.float32, smallest / len(shards), top_value / len(shards))
        return jnp.repeat(jnp.exp(heights), dims[position] // blocks).reshape((-1,) + (1,) * (len(dims) - position - 1))

    factor_of = one(*shards[0])
    for cut in shards[1:]:
        factor_of = factor_of * one(*cut)
    return factor_of


def centred(own_key, extent, width, most, pieces=(), held_as=jnp.bfloat16):
    drawn = jax.random.normal(own_key, extent, jnp.float32) * width
    if len(pieces) > 0:
        drawn = steps_of(own_key, extent, pieces, -0.22, 0.18) * drawn
    return jnp.clip(drawn, min=-most, max=most).astype(held_as)


def setup_inputs(seed: int = 0) -> dict:
    splits = jax.random.split(jax.random.key(seed), 5)
    plasma_state = centred(splits[0], (6, PLANES, ROWS, DEPTH), 0.5, 3.0, ((1, 8), (2, 64)), jnp.float32)
    right_side = draw_right_side(jax.random.fold_in(splits[4], 71), 0)
    resistivity = jnp.clip(jnp.exp(math.log(0.6) - 2.4849067 * jax.random.uniform(splits[2], (PLANES, ROWS, DEPTH), jnp.float32) ** steps_of(splits[2], (PLANES, ROWS, DEPTH), ((0, 8), (1, 64)), -0.2, 0.2)), 0.05, 0.6)
    jacobi_blocks = draw_jacobi_blocks(jax.random.fold_in(splits[4], 71), 0)
    return dict(plasma_state=plasma_state, right_side=right_side, resistivity=resistivity, jacobi_blocks=jacobi_blocks)


inverse_step = 1.0
viscosity = 0.2
epsilon = 1e-06

def neighbour(values, array_axis, offset, periodic):
    if periodic:
        return jnp.roll(values, -offset, array_axis)
    length = values.shape[array_axis]
    widths = [(0, 0)] * values.ndim
    widths[array_axis] = (1, 1)
    padded = jnp.pad(values, widths)
    return lax.slice_in_dim(padded, 1 + offset, 1 + offset + length, axis=array_axis)

def linear_flux(plasma, tangent, direction):
    magnetic = plasma[0:3]
    velocity = plasma[3:6]
    tang_mag = tangent[0:3]
    tang_vel = tangent[3:6]
    pressure = lax.optimization_barrier(jnp.sum(magnetic * tang_mag, axis=0))
    components = []
    for inner_index in range(3):
        components.append(tang_vel[direction] * magnetic[inner_index] + velocity[direction] * tang_mag[inner_index] - tang_mag[direction] * velocity[inner_index] - magnetic[direction] * tang_vel[inner_index])
    for inner_index in range(3):
        moment = tang_vel[direction] * velocity[inner_index] + velocity[direction] * tang_vel[inner_index] - tang_mag[direction] * magnetic[inner_index] - magnetic[direction] * tang_mag[inner_index]
        if inner_index == direction:
            moment = moment + pressure
        components.append(moment)
    return jnp.stack(components)

def diffusion_field(resistivity):
    shape = (3,) + resistivity.shape
    return jnp.concatenate([jnp.broadcast_to(resistivity[None], shape), jnp.full(shape, viscosity, jnp.float32)])

def jacobian_product(plasma, tangent, resistivity):
    result_sum = inverse_step * tangent
    laplace_sum = jnp.zeros_like(tangent)
    for direction, periodic in ((0, True), (1, False), (2, False)):
        flux_term = linear_flux(plasma, tangent, direction)
        result_sum = result_sum + 0.5 * (neighbour(flux_term, direction + 1, 1, periodic) - neighbour(flux_term, direction + 1, -1, periodic))
        laplace_sum = laplace_sum + neighbour(tangent, direction + 1, 1, periodic) + neighbour(tangent, direction + 1, -1, periodic) - 2.0 * tangent
    return result_sum - diffusion_field(resistivity) * laplace_sum

def precondition(blocks, vector):
    return jnp.einsum('abpqr,bpqr->apqr', blocks, vector.astype(jnp.float32), precision=lax.Precision.HIGHEST)

def least_squares(columns, initial_norm):
    count = len(columns)
    rhs_list = [initial_norm] + [jnp.float32(0.0)] * count
    cosines = []
    sines = []
    triangle = []
    estimate_list = []
    for column in range(count):
        entries = list(columns[column])
        for inner_index in range(column):
            first_value = entries[inner_index]
            second_value = entries[inner_index + 1]
            entries[inner_index] = cosines[inner_index] * first_value + sines[inner_index] * second_value
            entries[inner_index + 1] = -sines[inner_index] * first_value + cosines[inner_index] * second_value
        first_value = entries[column]
        second_value = entries[column + 1]
        radius = jnp.sqrt(first_value * first_value + second_value * second_value)
        cosine = first_value / radius
        sine_value = second_value / radius
        cosines.append(cosine)
        sines.append(sine_value)
        entries[column] = radius
        triangle.append(entries[:column + 1])
        previous = rhs_list[column]
        rhs_list[column] = cosine * previous
        rhs_list[column + 1] = -sine_value * previous
        estimate_list.append(jnp.abs(rhs_list[column + 1]))
    weights = [jnp.float32(0.0)] * count
    for column in reversed(range(count)):
        partial_value = rhs_list[column]
        for later in range(column + 1, count):
            partial_value = partial_value - triangle[later][column] * weights[later]
        weights[column] = partial_value / triangle[column][column]
    return (weights, estimate_list)

def reference(plasma_state, right_side, resistivity, jacobi_blocks):
    cell_count = 6 * PLANES * ROWS * DEPTH
    initial_norm = jnp.sqrt(jnp.sum(right_side * right_side) + epsilon)
    krylov_basis = [(right_side / initial_norm).astype(jnp.bfloat16)]
    directions = []
    columns = []
    for column in range(ITERS):
        tangent = precondition(jacobi_blocks, krylov_basis[column])
        image = jacobian_product(plasma_state, tangent, resistivity)
        directions.append(tangent)
        coefficients = [jnp.sum(image * earlier.astype(jnp.float32)) for earlier in krylov_basis]
        remainder = image
        for inner_index in range(column + 1):
            remainder = remainder - coefficients[inner_index] * krylov_basis[inner_index].astype(jnp.float32)
        new_norm = jnp.sqrt(jnp.sum(remainder * remainder) + epsilon)
        columns.append(coefficients + [new_norm])
        if column + 1 < ITERS:
            krylov_basis.append((remainder / new_norm).astype(jnp.bfloat16))
    weights, estimate_list = least_squares(columns, initial_norm)
    update = weights[0] * directions[0]
    for column in range(1, ITERS):
        update = update + weights[column] * directions[column]
    estimates = jnp.stack(estimate_list) / jnp.sqrt(jnp.float32(cell_count))
    return (update, estimates)
```

```python
import functools

import jax
import jax.numpy as jnp
from jax import lax
from jax.experimental import pallas as pl
from jax.experimental.pallas import tpu as pltpu
from jax.sharding import PartitionSpec as P

ITERS = 3
inverse_step = 1.0
viscosity = 0.2
epsilon = 1e-06

MESH = pl.DeviceIdType.MESH
F32 = jnp.float32
BF16 = jnp.bfloat16
PAIRS = [(i, j) for j in range(ITERS + 1) for i in range(j + 1)]
GROUP = 8


def flux(p, t, k):
    B, V, b, w = p[0:3], p[3:6], t[0:3], t[3:6]
    parts = []
    for i in range(3):
        parts.append(None if i == k else w[k] * B[i] + V[k] * b[i] - b[k] * V[i] - B[k] * w[i])
    for i in range(3):
        moment = w[k] * V[i] + V[k] * w[i] - b[k] * B[i] - B[k] * b[i]
        if i == k:
            moment = moment + (B[0] * b[0] + B[1] * b[1] + B[2] * b[2])
        parts.append(moment)
    return parts


def small_solve(gram, like):
    count = ITERS
    zero = jnp.zeros_like(like)
    norm0 = jnp.sqrt(gram[0][0] + epsilon)
    coefs = [[1.0 / norm0]]
    columns = []
    for j in range(count):
        shifted = [None] + coefs[j]
        size = j + 2
        applied = []
        for row in range(size):
            total = None
            for col in range(1, size):
                term = gram[row][col] * shifted[col]
                total = term if total is None else total + term
            applied.append(total)
        column = []
        for i in range(j + 1):
            total = None
            for row in range(i + 1):
                term = coefs[i][row] * applied[row]
                total = term if total is None else total + term
            column.append(total)
        remainder = []
        for row in range(size):
            total = shifted[row]
            for i in range(j + 1):
                if row <= i:
                    term = column[i] * coefs[i][row]
                    total = -term if total is None else total - term
            remainder.append(total)
        square = None
        for row in range(size):
            inner = None
            for col in range(size):
                term = gram[row][col] * remainder[col]
                inner = term if inner is None else inner + term
            term = inner * remainder[row]
            square = term if square is None else square + term
        norm = jnp.sqrt(jnp.maximum(square, 0.0) + epsilon)
        columns.append(column + [norm])
        if j + 1 < count:
            inverse = 1.0 / norm
            coefs.append([entry * inverse for entry in remainder])
    rhs = [norm0] + [zero] * count
    cosines, sines, triangle, estimates = [], [], [], []
    for column in range(count):
        entries = list(columns[column])
        for i in range(column):
            first, second = entries[i], entries[i + 1]
            entries[i] = cosines[i] * first + sines[i] * second
            entries[i + 1] = cosines[i] * second - sines[i] * first
        first, second = entries[column], entries[column + 1]
        radius = jnp.sqrt(first * first + second * second)
        inverse = 1.0 / radius
        cosine, sine = first * inverse, second * inverse
        cosines.append(cosine)
        sines.append(sine)
        triangle.append(entries[:column] + [inverse])
        previous = rhs[column]
        rhs[column] = cosine * previous
        rhs[column + 1] = -sine * previous
        estimates.append(jnp.abs(rhs[column + 1]))
    weights = [zero] * count
    for column in reversed(range(count)):
        value = rhs[column]
        for later in range(column + 1, count):
            value = value - triangle[later][column] * weights[later]
        weights[column] = value * triangle[column][column]
    alphas = []
    for row in range(count):
        total = None
        for j in range(row, count):
            term = weights[j] * coefs[j][row]
            total = term if total is None else total + term
        alphas.append(total)
    return alphas, estimates


def kernel(sizes, cell_count, plasma_hbm, right_hbm, resist_hbm, blocks_hbm, update_ref, est_ref,
           plasma, right, resist, blocks, w_ref, t_ref, up_ref, down_ref,
           tor_tx, tor_rx, pol_tx, pol_rx, sums,
           load_sem, tor_send, tor_recv, pol_send, pol_recv, sum_send, sum_recv):
    tors, pols = sizes
    tor = lax.axis_index("tor")
    pol = lax.axis_index("pol")
    tor_next, tor_prev = lax.rem(tor + 1, tors), lax.rem(tor + tors - 1, tors)
    pol_next, pol_prev = lax.rem(pol + 1, pols), lax.rem(pol + pols - 1, pols)
    outer, inner = pol // GROUP, lax.rem(pol, GROUP)

    def in_group(stage, rank):
        if stage == 0:
            return {"tor": rank, "pol": pol}
        if stage == 1:
            return {"tor": tor, "pol": outer * GROUP + rank}
        return {"tor": tor, "pol": rank * GROUP + inner}

    ranks = [tor, inner, outer]
    counts = [tors, GROUP, pols // GROUP]

    barrier = pltpu.get_barrier_semaphore()
    greeted = 0
    for stage in range(3):
        for step in range(1, counts[stage]):
            partner = lax.rem(ranks[stage] + step, counts[stage])
            pl.semaphore_signal(barrier, inc=1, device_id=in_group(stage, partner), device_id_type=MESH)
            greeted += 1
    for neighbour in (pol_next, pol_prev):
        pl.semaphore_signal(barrier, inc=1, device_id={"tor": tor, "pol": neighbour}, device_id_type=MESH)
        greeted += 1

    loads = [
        pltpu.make_async_copy(plasma_hbm, plasma, load_sem.at[0]),
        pltpu.make_async_copy(right_hbm, right, load_sem.at[1]),
        pltpu.make_async_copy(resist_hbm, resist, load_sem.at[2]),
    ]
    for row in range(6):
        loads.append(
            pltpu.make_async_copy(
                blocks_hbm.at[pl.ds(6 * row, 6)], blocks.at[pl.ds(6 * row, 6)], load_sem.at[3 + row]
            )
        )
    for load in loads:
        load.start()

    lane = lax.broadcasted_iota(jnp.int32, (8, 256), 1)
    sub = lax.broadcasted_iota(jnp.int32, (8, 256), 0)

    def up_depth(x):
        return jnp.where(lane == 255, 0.0, pltpu.roll(x, 255, 1))

    def down_depth(x):
        return jnp.where(lane == 0, 0.0, pltpu.roll(x, 1, 1))

    def up_row(x, halo):
        return jnp.where(sub == 7, jnp.broadcast_to(halo, (8, 256)), pltpu.roll(x, 7, 0))

    def down_row(x, halo):
        return jnp.where(sub == 0, jnp.broadcast_to(halo, (8, 256)), pltpu.roll(x, 1, 0))

    def tor_copies(slot):
        return [
            pltpu.make_async_remote_copy(
                src_ref=tor_tx.at[slot],
                dst_ref=tor_rx.at[slot, way],
                send_sem=tor_send.at[slot, way],
                recv_sem=tor_recv.at[slot, way],
                device_id={"tor": (tor_next, tor_prev)[way], "pol": pol},
                device_id_type=MESH,
            )
            for way in range(2)
        ]

    def pol_copies(slot):
        return [
            pltpu.make_async_remote_copy(
                src_ref=pol_tx.at[slot, way],
                dst_ref=pol_rx.at[slot, way],
                send_sem=pol_send.at[slot, way],
                recv_sem=pol_recv.at[slot, way],
                device_id={"tor": tor, "pol": (pol_next, pol_prev)[way]},
                device_id_type=MESH,
            )
            for way in range(2)
        ]

    def pack(slot, x):
        for c in range(6):
            pol_tx[slot, 0, c : c + 1, :] = x[c][7:8, :]
            pol_tx[slot, 1, c : c + 1, :] = x[c][0:1, :]
        for pair in range(3):
            tor_tx[slot, 16 * pair : 16 * pair + 16, :] = jnp.concatenate(
                [x[2 * pair], x[2 * pair + 1]], axis=0
            ).astype(BF16)

    def from_tor(slot, way):
        planes = []
        for pair in range(3):
            both = tor_rx[slot, way, 16 * pair : 16 * pair + 16, :].astype(F32)
            planes += [both[0:8], both[8:16]]
        return planes

    def precondition(vector):
        result = []
        for a in range(6):
            total = blocks[6 * a] * vector[0]
            for b in range(1, 6):
                total = total + blocks[6 * a + b] * vector[b]
            result.append(total)
        return result

    loads[0].wait()
    pack(3, [plasma[c] for c in range(6)])
    pl.semaphore_wait(barrier, greeted)
    flying = tor_copies(3) + pol_copies(3)
    for copy in flying:
        copy.start()
    for load in loads[1:]:
        load.wait()
    eta = resist[...]

    gram_rows = {}

    def product(i, j):
        total = None
        for c in range(6):
            term = w_ref[i, c] * w_ref[j, c]
            total = term if total is None else total + term
        total = total[:, 0:128] + total[:, 128:256]
        gram_rows[(i, j)] = jnp.sum(total, axis=0, keepdims=True)

    for c in range(6):
        w_ref[0, c] = right[c]

    for k in range(ITERS):
        t = precondition([w_ref[k, c] for c in range(6)])
        for c in range(6):
            t_ref[k, c] = t[c]
        pack(k, t)
        tor_moves, pol_moves = tor_copies(k), pol_copies(k)
        for copy in pol_moves + tor_moves:
            copy.start()
        flying += pol_moves + tor_moves
        p = [plasma[c] for c in range(6)]
        f = flux(p, t, 2)
        partial = []
        for c in range(6):
            coefficient = eta if c < 3 else viscosity
            total = inverse_step * t[c] + coefficient * (6.0 * t[c] - up_depth(t[c]) - down_depth(t[c]))
            if f[c] is not None:
                half = 0.5 * f[c]
                total = total + (up_depth(half) - down_depth(half))
            partial.append(total)
        for i in range(k + 1):
            product(i, k)
        if k == 0:
            for copy in flying[0:4]:
                copy.wait_recv()
            for c in range(6):
                up_ref[c] = up_row(plasma[c], pol_rx[3, 1, c : c + 1, :])
                down_ref[c] = down_row(plasma[c], pol_rx[3, 0, c : c + 1, :])
        for copy in pol_moves:
            copy.wait_recv()
        t_up = [
            up_row(t[c], jnp.where(pol == pols - 1, 0.0, pol_rx[k, 1, c : c + 1, :])) for c in range(6)
        ]
        t_down = [down_row(t[c], jnp.where(pol == 0, 0.0, pol_rx[k, 0, c : c + 1, :])) for c in range(6)]
        f_up = flux([up_ref[c] for c in range(6)], t_up, 1)
        f_down = flux([down_ref[c] for c in range(6)], t_down, 1)
        for c in range(6):
            coefficient = eta if c < 3 else viscosity
            partial[c] = partial[c] - coefficient * (t_up[c] + t_down[c])
            if f_up[c] is not None:
                partial[c] = partial[c] + 0.5 * (f_up[c] - f_down[c])
        for copy in tor_moves:
            copy.wait_recv()
        t_up, t_down = from_tor(k, 1), from_tor(k, 0)
        f_up = flux(from_tor(3, 1), t_up, 0)
        f_down = flux(from_tor(3, 0), t_down, 0)
        for c in range(6):
            coefficient = eta if c < 3 else viscosity
            total = partial[c] - coefficient * (t_up[c] + t_down[c])
            if f_up[c] is not None:
                total = total + 0.5 * (f_up[c] - f_down[c])
            w_ref[k + 1, c] = total

    for i in range(ITERS + 1):
        product(i, ITERS)

    wide_lane = lax.broadcasted_iota(jnp.int32, (16, 128), 1)
    wide_sub = lax.broadcasted_iota(jnp.int32, (16, 128), 0)
    rows = jnp.zeros((16, 128), F32)
    for index, pair in enumerate(PAIRS):
        rows = jnp.where(wide_sub == index, jnp.broadcast_to(gram_rows[pair], (16, 128)), rows)
    rows = jnp.broadcast_to(jnp.sum(rows, axis=1, keepdims=True), (16, 128))
    mine = jnp.sum(jnp.where(wide_lane == wide_sub, rows, 0.0), axis=0, keepdims=True)

    for stage in range(3):
        sums[stage, ranks[stage]] = mine
        moves = []
        for step in range(1, counts[stage]):
            partner = lax.rem(ranks[stage] + step, counts[stage])
            moves.append(
                pltpu.make_async_remote_copy(
                    src_ref=sums.at[stage, ranks[stage]],
                    dst_ref=sums.at[stage, ranks[stage]],
                    send_sem=sum_send.at[stage, step],
                    recv_sem=sum_recv.at[stage, step],
                    device_id=in_group(stage, partner),
                    device_id_type=MESH,
                )
            )
        for copy in moves:
            copy.start()
        flying += moves
        for copy in moves:
            copy.wait_recv()
        mine = sums[stage, 0]
        for rank in range(1, counts[stage]):
            mine = mine + sums[stage, rank]

    row_lane = lax.broadcasted_iota(jnp.int32, (1, 128), 1)
    gram = [[None] * (ITERS + 1) for _ in range(ITERS + 1)]
    for index, (i, j) in enumerate(PAIRS):
        entry = jnp.sum(jnp.where(row_lane == index, mine, 0.0), axis=1, keepdims=True)
        entry = jnp.broadcast_to(entry, (1, 128))
        gram[i][j] = entry
        gram[j][i] = entry
    alphas, estimates = small_solve(gram, gram[0][0])
    scale = 1.0 / float(cell_count) ** 0.5
    est = jnp.zeros((1, 128), F32)
    for index in range(ITERS):
        est = jnp.where(row_lane == index, estimates[index] * scale, est)
    est_ref[...] = est
    full = [jnp.broadcast_to(jnp.concatenate([a, a], axis=1), (8, 256)) for a in alphas]
    for c in range(6):
        update_ref[c] = full[0] * t_ref[0, c] + full[1] * t_ref[1, c] + full[2] * t_ref[2, c]
    for copy in flying:
        copy.wait_send()


def solution(mesh):
    sizes = (mesh.shape["tor"], mesh.shape["pol"])

    def shards(plasma_state, right_side, resistivity, jacobi_blocks):
        cell_count = plasma_state.size * sizes[0] * sizes[1]
        hbm = pl.BlockSpec(memory_space=pl.ANY)
        vmem = pl.BlockSpec(memory_space=pltpu.VMEM)
        update, est = pl.pallas_call(
            functools.partial(kernel, sizes, cell_count),
            out_shape=(jax.ShapeDtypeStruct((6, 8, 256), F32), jax.ShapeDtypeStruct((1, 128), F32)),
            in_specs=[hbm] * 4,
            out_specs=(vmem, vmem),
            scratch_shapes=[
                pltpu.VMEM((6, 8, 256), F32),
                pltpu.VMEM((6, 8, 256), F32),
                pltpu.VMEM((8, 256), F32),
                pltpu.VMEM((36, 8, 256), F32),
                pltpu.VMEM((ITERS + 1, 6, 8, 256), F32),
                pltpu.VMEM((ITERS, 6, 8, 256), F32),
                pltpu.VMEM((6, 8, 256), F32),
                pltpu.VMEM((6, 8, 256), F32),
                pltpu.VMEM((4, 48, 256), BF16),
                pltpu.VMEM((4, 2, 48, 256), BF16),
                pltpu.VMEM((4, 2, 6, 256), F32),
                pltpu.VMEM((4, 2, 6, 256), F32),
                pltpu.VMEM((3, GROUP, 1, 128), F32),
                pltpu.SemaphoreType.DMA((9,)),
                pltpu.SemaphoreType.DMA((4, 2)),
                pltpu.SemaphoreType.DMA((4, 2)),
                pltpu.SemaphoreType.DMA((4, 2)),
                pltpu.SemaphoreType.DMA((4, 2)),
                pltpu.SemaphoreType.DMA((3, GROUP)),
                pltpu.SemaphoreType.DMA((3, GROUP)),
            ],
            compiler_params=pltpu.CompilerParams(collective_id=0, has_side_effects=True),
            name="gmres",
        )(
            plasma_state.reshape(6, 8, 256),
            right_side.reshape(6, 8, 256),
            resistivity.reshape(8, 256),
            jacobi_blocks.reshape(36, 8, 256),
        )
        return update.reshape(6, 1, 8, 256), est[0, :ITERS]

    return jax.shard_map(
        shards,
        mesh=mesh,
        in_specs=(
            P(None, "tor", "pol", None),
            P(None, "tor", "pol", None),
            P("tor", "pol", None),
            P(None, None, "tor", "pol", None),
        ),
        out_specs=(P(None, "tor", "pol", None), P()),
        check_vma=False,
    )
```

```python
import functools

import jax
import jax.numpy as jnp
from jax import lax
from jax.experimental import pallas as pl
from jax.experimental.pallas import tpu as pltpu
from jax.sharding import PartitionSpec as P

ITERS = 3
inverse_step = 1.0
viscosity = 0.2
epsilon = 1e-06

MESH = pl.DeviceIdType.MESH
F32 = jnp.float32
BF16 = jnp.bfloat16
PAIRS = [(i, j) for j in range(ITERS + 1) for i in range(j + 1)]
GROUP = 8


def flux(p, t, k):
    B, V, b, w = p[0:3], p[3:6], t[0:3], t[3:6]
    parts = []
    for i in range(3):
        parts.append(None if i == k else w[k] * B[i] + V[k] * b[i] - b[k] * V[i] - B[k] * w[i])
    for i in range(3):
        moment = w[k] * V[i] + V[k] * w[i] - b[k] * B[i] - B[k] * b[i]
        if i == k:
            moment = moment + (B[0] * b[0] + B[1] * b[1] + B[2] * b[2])
        parts.append(moment)
    return parts


def small_solve(gram, like):
    count = ITERS
    zero = jnp.zeros_like(like)
    norm0 = jnp.sqrt(gram[0][0] + epsilon)
    coefs = [[1.0 / norm0]]
    columns = []
    for j in range(count):
        shifted = [None] + coefs[j]
        size = j + 2
        applied = []
        for row in range(size):
            total = None
            for col in range(1, size):
                term = gram[row][col] * shifted[col]
                total = term if total is None else total + term
            applied.append(total)
        column = []
        for i in range(j + 1):
            total = None
            for row in range(i + 1):
                term = coefs[i][row] * applied[row]
                total = term if total is None else total + term
            column.append(total)
        remainder = []
        for row in range(size):
            total = shifted[row]
            for i in range(j + 1):
                if row <= i:
                    term = column[i] * coefs[i][row]
                    total = -term if total is None else total - term
            remainder.append(total)
        square = None
        for row in range(size):
            inner = None
            for col in range(size):
                term = gram[row][col] * remainder[col]
                inner = term if inner is None else inner + term
            term = inner * remainder[row]
            square = term if square is None else square + term
        norm = jnp.sqrt(jnp.maximum(square, 0.0) + epsilon)
        columns.append(column + [norm])
        if j + 1 < count:
            inverse = 1.0 / norm
            coefs.append([entry * inverse for entry in remainder])
    rhs = [norm0] + [zero] * count
    cosines, sines, triangle, estimates = [], [], [], []
    for column in range(count):
        entries = list(columns[column])
        for i in range(column):
            first, second = entries[i], entries[i + 1]
            entries[i] = cosines[i] * first + sines[i] * second
            entries[i + 1] = cosines[i] * second - sines[i] * first
        first, second = entries[column], entries[column + 1]
        radius = jnp.sqrt(first * first + second * second)
        inverse = 1.0 / radius
        cosine, sine = first * inverse, second * inverse
        cosines.append(cosine)
        sines.append(sine)
        triangle.append(entries[:column] + [inverse])
        previous = rhs[column]
        rhs[column] = cosine * previous
        rhs[column + 1] = -sine * previous
        estimates.append(jnp.abs(rhs[column + 1]))
    weights = [zero] * count
    for column in reversed(range(count)):
        value = rhs[column]
        for later in range(column + 1, count):
            value = value - triangle[later][column] * weights[later]
        weights[column] = value * triangle[column][column]
    alphas = []
    for row in range(count):
        total = None
        for j in range(row, count):
            term = weights[j] * coefs[j][row]
            total = term if total is None else total + term
        alphas.append(total)
    return alphas, estimates


def kernel(sizes, plasma_hbm, right_hbm, resist_hbm, blocks_hbm, t_ref, total_ref,
           plasma, right, resist, blocks, w_ref, up_ref, down_ref,
           tor_tx, tor_rx, pol_tx, pol_rx, mine_ref, back_ref, member_sums, leader_sums,
           load_sem, tor_send, tor_recv, pol_send, pol_recv,
           member_send, member_recv, leader_send, leader_recv, back_send, back_recv):
    tors, pols = sizes
    halves = 2
    width = tors // halves
    columns = pols // GROUP
    members = halves * GROUP
    leaders = width * columns
    tor = lax.axis_index("tor")
    pol = lax.axis_index("pol")
    tor_next, tor_prev = lax.rem(tor + 1, tors), lax.rem(tor + tors - 1, tors)
    pol_next, pol_prev = lax.rem(pol + 1, pols), lax.rem(pol + pols - 1, pols)

    half, lead_tor = tor // width, lax.rem(tor, width)
    column, inner = pol // GROUP, lax.rem(pol, GROUP)
    member = half * GROUP + inner
    leader = lead_tor * columns + column
    is_leader = member == 1
    to_leader = {"tor": lead_tor, "pol": column * GROUP + 1}

    def member_at(index):
        return {"tor": (index // GROUP) * width + lead_tor, "pol": column * GROUP + index % GROUP}

    def leader_at(index):
        return {"tor": index // columns, "pol": lax.rem(index, columns) * GROUP + 1}

    others = [m for m in range(members) if m != 1]

    loads = [
        pltpu.make_async_copy(plasma_hbm, plasma, load_sem.at[0]),
        pltpu.make_async_copy(right_hbm, right, load_sem.at[1]),
        pltpu.make_async_copy(resist_hbm, resist, load_sem.at[2]),
    ]
    for row in range(6):
        loads.append(
            pltpu.make_async_copy(
                blocks_hbm.at[pl.ds(6 * row, 6)], blocks.at[pl.ds(6 * row, 6)], load_sem.at[3 + row]
            )
        )
    for load in loads:
        load.start()

    barrier = pltpu.get_barrier_semaphore()
    for neighbour in (pol_next, pol_prev):
        pl.semaphore_signal(barrier, inc=1, device_id={"tor": tor, "pol": neighbour}, device_id_type=MESH)
    for neighbour in (tor_next, tor_prev):
        pl.semaphore_signal(barrier, inc=1, device_id={"tor": neighbour, "pol": pol}, device_id_type=MESH)

    @pl.when(is_leader)
    def _():
        for index in others:
            pl.semaphore_signal(barrier, inc=1, device_id=member_at(index), device_id_type=MESH)
        for step in range(1, leaders):
            partner = leader_at(lax.rem(leader + step, leaders))
            pl.semaphore_signal(barrier, inc=1, device_id=partner, device_id_type=MESH)

    lane = lax.broadcasted_iota(jnp.int32, (8, 256), 1)
    sub = lax.broadcasted_iota(jnp.int32, (8, 256), 0)

    def up_depth(x):
        return jnp.where(lane == 255, 0.0, pltpu.roll(x, 255, 1))

    def down_depth(x):
        return jnp.where(lane == 0, 0.0, pltpu.roll(x, 1, 1))

    def up_row(x, halo):
        return jnp.where(sub == 7, jnp.broadcast_to(halo, (8, 256)), pltpu.roll(x, 7, 0))

    def down_row(x, halo):
        return jnp.where(sub == 0, jnp.broadcast_to(halo, (8, 256)), pltpu.roll(x, 1, 0))

    def tor_copies(slot):
        return [
            pltpu.make_async_remote_copy(
                src_ref=tor_tx.at[slot],
                dst_ref=tor_rx.at[slot, way],
                send_sem=tor_send.at[slot, way],
                recv_sem=tor_recv.at[slot, way],
                device_id={"tor": (tor_next, tor_prev)[way], "pol": pol},
                device_id_type=MESH,
            )
            for way in range(2)
        ]

    def pol_copies(slot):
        return [
            pltpu.make_async_remote_copy(
                src_ref=pol_tx.at[slot, way],
                dst_ref=pol_rx.at[slot, way],
                send_sem=pol_send.at[slot, way],
                recv_sem=pol_recv.at[slot, way],
                device_id={"tor": tor, "pol": (pol_next, pol_prev)[way]},
                device_id_type=MESH,
            )
            for way in range(2)
        ]

    def pack(slot, x):
        for c in range(6):
            pol_tx[slot, 0, c : c + 1, :] = x[c][7:8, :]
            pol_tx[slot, 1, c : c + 1, :] = x[c][0:1, :]
        for pair in range(3):
            tor_tx[slot, 16 * pair : 16 * pair + 16, :] = jnp.concatenate(
                [x[2 * pair], x[2 * pair + 1]], axis=0
            ).astype(BF16)

    def from_tor(slot, way):
        planes = []
        for pair in range(3):
            both = tor_rx[slot, way, 16 * pair : 16 * pair + 16, :].astype(F32)
            planes += [both[0:8], both[8:16]]
        return planes

    loads[0].wait()
    pack(3, [plasma[c] for c in range(6)])
    loads[1].wait()
    for c in range(6):
        w_ref[0, c] = right[c]

    def precondition(k):
        vector = [w_ref[k, c] for c in range(6)]
        result = []
        for a in range(6):
            if k == 0:
                loads[3 + a].wait()
            total = blocks[6 * a] * vector[0]
            for b in range(1, 6):
                total = total + blocks[6 * a + b] * vector[b]
            result.append(total)
        return result

    flying = []
    gram_rows = {}

    def product(i, j):
        total = None
        for c in range(6):
            term = w_ref[i, c] * w_ref[j, c]
            total = term if total is None else total + term
        total = total[:, 0:128] + total[:, 128:256]
        gram_rows[(i, j)] = jnp.sum(total, axis=0, keepdims=True)

    for k in range(ITERS):
        t = precondition(k)
        pack(k, t)
        tor_moves, pol_moves = tor_copies(k), pol_copies(k)
        if k == 0:

            @pl.when(is_leader)
            def _():
                pl.semaphore_wait(barrier, 4 + leaders - 1)

            @pl.when(jnp.logical_not(is_leader))
            def _():
                pl.semaphore_wait(barrier, 4 + 1)

        for copy in pol_moves + tor_moves:
            copy.start()
        if k == 0:
            state_moves = pol_copies(3) + tor_copies(3)
            for copy in state_moves:
                copy.start()
            flying += state_moves
        flying += pol_moves + tor_moves
        for c in range(6):
            t_ref[k, c] = t[c]
        if k == 0:
            loads[2].wait()
        eta = resist[...]
        p = [plasma[c] for c in range(6)]
        f = flux(p, t, 2)
        partial = []
        for c in range(6):
            coefficient = eta if c < 3 else viscosity
            total = inverse_step * t[c] + coefficient * (6.0 * t[c] - up_depth(t[c]) - down_depth(t[c]))
            if f[c] is not None:
                half_flux = 0.5 * f[c]
                total = total + (up_depth(half_flux) - down_depth(half_flux))
            partial.append(total)
        for i in range(k + 1):
            product(i, k)
        if k == 0:
            for copy in state_moves:
                copy.wait_recv()
            for c in range(6):
                up_ref[c] = up_row(plasma[c], pol_rx[3, 1, c : c + 1, :])
                down_ref[c] = down_row(plasma[c], pol_rx[3, 0, c : c + 1, :])
        for copy in pol_moves:
            copy.wait_recv()
        t_up = [
            up_row(t[c], jnp.where(pol == pols - 1, 0.0, pol_rx[k, 1, c : c + 1, :])) for c in range(6)
        ]
        t_down = [down_row(t[c], jnp.where(pol == 0, 0.0, pol_rx[k, 0, c : c + 1, :])) for c in range(6)]
        f_up = flux([up_ref[c] for c in range(6)], t_up, 1)
        f_down = flux([down_ref[c] for c in range(6)], t_down, 1)
        for c in range(6):
            coefficient = eta if c < 3 else viscosity
            partial[c] = partial[c] - coefficient * (t_up[c] + t_down[c])
            if f_up[c] is not None:
                partial[c] = partial[c] + 0.5 * (f_up[c] - f_down[c])
        for copy in tor_moves:
            copy.wait_recv()
        t_up, t_down = from_tor(k, 1), from_tor(k, 0)
        f_up = flux(from_tor(3, 1), t_up, 0)
        f_down = flux(from_tor(3, 0), t_down, 0)
        for c in range(6):
            coefficient = eta if c < 3 else viscosity
            total = partial[c] - coefficient * (t_up[c] + t_down[c])
            if f_up[c] is not None:
                total = total + 0.5 * (f_up[c] - f_down[c])
            w_ref[k + 1, c] = total

    for i in range(ITERS + 1):
        product(i, ITERS)

    wide_lane = lax.broadcasted_iota(jnp.int32, (16, 128), 1)
    wide_sub = lax.broadcasted_iota(jnp.int32, (16, 128), 0)
    rows = jnp.zeros((16, 128), F32)
    for index, pair in enumerate(PAIRS):
        rows = jnp.where(wide_sub == index, jnp.broadcast_to(gram_rows[pair], (16, 128)), rows)
    rows = jnp.broadcast_to(jnp.sum(rows, axis=1, keepdims=True), (16, 128))
    mine = jnp.sum(jnp.where(wide_lane == wide_sub, rows, 0.0), axis=0, keepdims=True)

    def tree(values):
        while len(values) > 1:
            values = [a + b for a, b in zip(values[0::2], values[1::2])]
        return values[0]

    def to_member(index):
        return pltpu.make_async_remote_copy(
            src_ref=mine_ref,
            dst_ref=back_ref,
            send_sem=back_send.at[index],
            recv_sem=back_recv,
            device_id=member_at(index),
            device_id_type=MESH,
        )

    def member_copy(index):
        return pltpu.make_async_remote_copy(
            src_ref=mine_ref,
            dst_ref=member_sums.at[index],
            send_sem=member_send,
            recv_sem=member_recv.at[index],
            device_id=to_leader,
            device_id_type=MESH,
        )

    @pl.when(jnp.logical_not(is_leader))
    def _():
        mine_ref[...] = mine
        upward = member_copy(member)
        upward.start()
        upward.wait_send()
        to_member(0).wait_recv()
        total_ref[...] = back_ref[...]

    @pl.when(is_leader)
    def _():
        member_sums[1] = mine
        for index in others:
            member_copy(index).wait_recv()
        leader_sums[leader] = tree([member_sums[m] for m in range(members)])
        moves = [
            pltpu.make_async_remote_copy(
                src_ref=leader_sums.at[leader],
                dst_ref=leader_sums.at[leader],
                send_sem=leader_send.at[step],
                recv_sem=leader_recv.at[step],
                device_id=leader_at(lax.rem(leader + step, leaders)),
                device_id_type=MESH,
            )
            for step in range(1, leaders)
        ]
        for copy in moves:
            copy.start()
        for copy in moves:
            copy.wait_recv()
        total = tree([leader_sums[m] for m in range(leaders)])
        mine_ref[...] = total
        backs = [to_member(index) for index in others]
        for copy in backs:
            copy.start()
        total_ref[...] = total
        for copy in moves + backs:
            copy.wait_send()

    for copy in flying:
        copy.wait_send()


def combine(cell_count, t_ref, total_ref, update_ref, est_ref):
    mine = total_ref[...]
    row_lane = lax.broadcasted_iota(jnp.int32, (1, 128), 1)
    gram = [[None] * (ITERS + 1) for _ in range(ITERS + 1)]
    for index, (i, j) in enumerate(PAIRS):
        entry = jnp.sum(jnp.where(row_lane == index, mine, 0.0), axis=1, keepdims=True)
        entry = jnp.broadcast_to(entry, (1, 128))
        gram[i][j] = entry
        gram[j][i] = entry
    alphas, estimates = small_solve(gram, gram[0][0])
    scale = 1.0 / float(cell_count) ** 0.5
    est = jnp.zeros((1, 128), F32)
    for index in range(ITERS):
        est = jnp.where(row_lane == index, estimates[index] * scale, est)
    est_ref[...] = est[0, 0:ITERS]
    full = [jnp.broadcast_to(jnp.concatenate([a, a], axis=1), (8, 256)) for a in alphas]
    for c in range(6):
        update_ref[c] = full[0] * t_ref[0, c] + full[1] * t_ref[1, c] + full[2] * t_ref[2, c]


def solution(mesh):
    sizes = (mesh.shape["tor"], mesh.shape["pol"])

    def shards(plasma_state, right_side, resistivity, jacobi_blocks):
        cell_count = plasma_state.size * sizes[0] * sizes[1]
        hbm = pl.BlockSpec(memory_space=pl.ANY)
        vmem = pl.BlockSpec(memory_space=pltpu.VMEM)
        tangents, total = pl.pallas_call(
            functools.partial(kernel, sizes),
            out_shape=(pltpu.VMEM((ITERS, 6, 8, 256), F32), pltpu.VMEM((1, 128), F32)),
            in_specs=[hbm] * 4,
            out_specs=(vmem, vmem),
            scratch_shapes=[
                pltpu.VMEM((6, 8, 256), F32),
                pltpu.VMEM((6, 8, 256), F32),
                pltpu.VMEM((8, 256), F32),
                pltpu.VMEM((36, 8, 256), F32),
                pltpu.VMEM((ITERS + 1, 6, 8, 256), F32),
                pltpu.VMEM((6, 8, 256), F32),
                pltpu.VMEM((6, 8, 256), F32),
                pltpu.VMEM((4, 48, 256), BF16),
                pltpu.VMEM((4, 2, 48, 256), BF16),
                pltpu.VMEM((4, 2, 6, 256), F32),
                pltpu.VMEM((4, 2, 6, 256), F32),
                pltpu.VMEM((1, 128), F32),
                pltpu.VMEM((1, 128), F32),
                pltpu.VMEM((16, 1, 128), F32),
                pltpu.VMEM((32, 1, 128), F32),
                pltpu.SemaphoreType.DMA((9,)),
                pltpu.SemaphoreType.DMA((4, 2)),
                pltpu.SemaphoreType.DMA((4, 2)),
                pltpu.SemaphoreType.DMA((4, 2)),
                pltpu.SemaphoreType.DMA((4, 2)),
                pltpu.SemaphoreType.DMA,
                pltpu.SemaphoreType.DMA((16,)),
                pltpu.SemaphoreType.DMA((32,)),
                pltpu.SemaphoreType.DMA((32,)),
                pltpu.SemaphoreType.DMA((16,)),
                pltpu.SemaphoreType.DMA,
            ],
            compiler_params=pltpu.CompilerParams(collective_id=0, has_side_effects=True),
            name="krylov",
        )(
            plasma_state.reshape(6, 8, 256),
            right_side.reshape(6, 8, 256),
            resistivity.reshape(8, 256),
            jacobi_blocks.reshape(36, 8, 256),
        )
        update, est = pl.pallas_call(
            functools.partial(combine, cell_count),
            out_shape=(jax.ShapeDtypeStruct((6, 8, 256), F32), jax.ShapeDtypeStruct((ITERS,), F32)),
            in_specs=[vmem] * 2,
            out_specs=(vmem, vmem),
            name="combine",
        )(
            pltpu.with_memory_space_constraint(tangents, pltpu.VMEM),
            pltpu.with_memory_space_constraint(total, pltpu.VMEM),
        )
        return update.reshape(6, 1, 8, 256), est

    return jax.shard_map(
        shards,
        mesh=mesh,
        in_specs=(
            P(None, "tor", "pol", None),
            P(None, "tor", "pol", None),
            P("tor", "pol", None),
            P(None, None, "tor", "pol", None),
        ),
        out_specs=(P(None, "tor", "pol", None), P()),
        check_vma=False,
    )
```

```python
import functools

import jax
import jax.numpy as jnp
from jax import lax
from jax.experimental import pallas as pl
from jax.experimental.pallas import tpu as pltpu
from jax.sharding import PartitionSpec as P

ITERS = 3
inverse_step = 1.0
viscosity = 0.2
epsilon = 1e-06

MESH = pl.DeviceIdType.MESH
F32 = jnp.float32
BF16 = jnp.bfloat16
PAIRS = [(i, j) for j in range(ITERS + 1) for i in range(j + 1)]
GROUP = 8


def flux(p, t, k):
    B, V, b, w = p[0:3], p[3:6], t[0:3], t[3:6]
    parts = []
    for i in range(3):
        parts.append(None if i == k else w[k] * B[i] + V[k] * b[i] - b[k] * V[i] - B[k] * w[i])
    for i in range(3):
        moment = w[k] * V[i] + V[k] * w[i] - b[k] * B[i] - B[k] * b[i]
        if i == k:
            moment = moment + (B[0] * b[0] + B[1] * b[1] + B[2] * b[2])
        parts.append(moment)
    return parts


def small_solve(gram, like):
    count = ITERS
    zero = jnp.zeros_like(like)
    norm0 = jnp.sqrt(gram[0][0] + epsilon)
    coefs = [[1.0 / norm0]]
    columns = []
    for j in range(count):
        shifted = [None] + coefs[j]
        size = j + 2
        applied = []
        for row in range(size):
            total = None
            for col in range(1, size):
                term = gram[row][col] * shifted[col]
                total = term if total is None else total + term
            applied.append(total)
        column = []
        for i in range(j + 1):
            total = None
            for row in range(i + 1):
                term = coefs[i][row] * applied[row]
                total = term if total is None else total + term
            column.append(total)
        remainder = []
        for row in range(size):
            total = shifted[row]
            for i in range(j + 1):
                if row <= i:
                    term = column[i] * coefs[i][row]
                    total = -term if total is None else total - term
            remainder.append(total)
        square = None
        for row in range(size):
            inner = None
            for col in range(size):
                term = gram[row][col] * remainder[col]
                inner = term if inner is None else inner + term
            term = inner * remainder[row]
            square = term if square is None else square + term
        norm = jnp.sqrt(jnp.maximum(square, 0.0) + epsilon)
        columns.append(column + [norm])
        if j + 1 < count:
            inverse = 1.0 / norm
            coefs.append([entry * inverse for entry in remainder])
    rhs = [norm0] + [zero] * count
    cosines, sines, triangle, estimates = [], [], [], []
    for column in range(count):
        entries = list(columns[column])
        for i in range(column):
            first, second = entries[i], entries[i + 1]
            entries[i] = cosines[i] * first + sines[i] * second
            entries[i + 1] = cosines[i] * second - sines[i] * first
        first, second = entries[column], entries[column + 1]
        radius = jnp.sqrt(first * first + second * second)
        inverse = 1.0 / radius
        cosine, sine = first * inverse, second * inverse
        cosines.append(cosine)
        sines.append(sine)
        triangle.append(entries[:column] + [inverse])
        previous = rhs[column]
        rhs[column] = cosine * previous
        rhs[column + 1] = -sine * previous
        estimates.append(jnp.abs(rhs[column + 1]))
    weights = [zero] * count
    for column in reversed(range(count)):
        value = rhs[column]
        for later in range(column + 1, count):
            value = value - triangle[later][column] * weights[later]
        weights[column] = value * triangle[column][column]
    alphas = []
    for row in range(count):
        total = None
        for j in range(row, count):
            term = weights[j] * coefs[j][row]
            total = term if total is None else total + term
        alphas.append(total)
    return alphas, estimates


def kernel(sizes, scale, plasma_hbm, right_hbm, resist_hbm, blocks_hbm, t_ref, weights_ref,
           plasma, right, resist, blocks, w_ref, up_ref, down_ref,
           tor_tx, tor_rx, pol_tx, pol_rx, mine_ref, back_ref, sum_ref, all_sums,
           load_sem, tor_send, tor_recv, pol_send, pol_recv,
           root_send, root_recv, back_send, back_recv):
    tors, pols = sizes
    halves = 2
    width = tors // halves
    columns = pols // GROUP
    members = halves * GROUP
    leaders = width * columns
    tor = lax.axis_index("tor")
    pol = lax.axis_index("pol")
    tor_next, tor_prev = lax.rem(tor + 1, tors), lax.rem(tor + tors - 1, tors)
    pol_next, pol_prev = lax.rem(pol + 1, pols), lax.rem(pol + pols - 1, pols)

    half, lead_tor = tor // width, lax.rem(tor, width)
    column, inner = pol // GROUP, lax.rem(pol, GROUP)
    member = half * GROUP + inner
    leader = lead_tor * columns + column
    is_leader = member == 1
    to_leader = {"tor": lead_tor, "pol": column * GROUP + 1}

    def member_at(index):
        return {"tor": (index // GROUP) * width + lead_tor, "pol": column * GROUP + index % GROUP}

    def leader_at(index):
        return {"tor": index // columns, "pol": lax.rem(index, columns) * GROUP + 1}

    others = [m for m in range(members) if m != 1]

    barrier = pltpu.get_barrier_semaphore()
    for neighbour in (pol_next, pol_prev):
        pl.semaphore_signal(barrier, inc=1, device_id={"tor": tor, "pol": neighbour}, device_id_type=MESH)
    for neighbour in (tor_next, tor_prev):
        pl.semaphore_signal(barrier, inc=1, device_id={"tor": neighbour, "pol": pol}, device_id_type=MESH)

    loads = [
        pltpu.make_async_copy(plasma_hbm, plasma, load_sem.at[0]),
        pltpu.make_async_copy(right_hbm, right, load_sem.at[1]),
        pltpu.make_async_copy(resist_hbm, resist, load_sem.at[2]),
    ]
    for row in range(6):
        loads.append(
            pltpu.make_async_copy(
                blocks_hbm.at[pl.ds(6 * row, 6)], blocks.at[pl.ds(6 * row, 6)], load_sem.at[3 + row]
            )
        )
    for load in loads:
        load.start()

    @pl.when(is_leader)
    def _():
        for step in range(1, leaders):
            partner = leader_at(lax.rem(leader + step, leaders))
            pl.semaphore_signal(barrier, inc=1, device_id=partner, device_id_type=MESH)
        pl.semaphore_wait(barrier, 4 + leaders - 1)
        for index in others:
            pl.semaphore_signal(barrier, inc=1, device_id=member_at(index), device_id_type=MESH)

    lane = lax.broadcasted_iota(jnp.int32, (8, 256), 1)
    sub = lax.broadcasted_iota(jnp.int32, (8, 256), 0)

    def up_depth(x):
        return jnp.where(lane == 255, 0.0, pltpu.roll(x, 255, 1))

    def down_depth(x):
        return jnp.where(lane == 0, 0.0, pltpu.roll(x, 1, 1))

    def up_row(x, halo):
        return jnp.where(sub == 7, jnp.broadcast_to(halo, (8, 256)), pltpu.roll(x, 7, 0))

    def down_row(x, halo):
        return jnp.where(sub == 0, jnp.broadcast_to(halo, (8, 256)), pltpu.roll(x, 1, 0))

    def tor_copies(slot):
        return [
            pltpu.make_async_remote_copy(
                src_ref=tor_tx.at[slot],
                dst_ref=tor_rx.at[slot, way],
                send_sem=tor_send.at[slot, way],
                recv_sem=tor_recv.at[slot, way],
                device_id={"tor": (tor_next, tor_prev)[way], "pol": pol},
                device_id_type=MESH,
            )
            for way in range(2)
        ]

    def pol_copies(slot):
        return [
            pltpu.make_async_remote_copy(
                src_ref=pol_tx.at[slot, way],
                dst_ref=pol_rx.at[slot, way],
                send_sem=pol_send.at[slot, way],
                recv_sem=pol_recv.at[slot, way],
                device_id={"tor": tor, "pol": (pol_next, pol_prev)[way]},
                device_id_type=MESH,
            )
            for way in range(2)
        ]

    def pack(slot, x):
        for c in range(6):
            pol_tx[slot, 0, c : c + 1, :] = x[c][7:8, :]
            pol_tx[slot, 1, c : c + 1, :] = x[c][0:1, :]
        for pair in range(3):
            tor_tx[slot, 16 * pair : 16 * pair + 16, :] = jnp.concatenate(
                [x[2 * pair], x[2 * pair + 1]], axis=0
            ).astype(BF16)

    def from_tor(slot, way):
        planes = []
        for pair in range(3):
            both = tor_rx[slot, way, 16 * pair : 16 * pair + 16, :].astype(F32)
            planes += [both[0:8], both[8:16]]
        return planes

    loads[0].wait()
    pack(3, [plasma[c] for c in range(6)])
    loads[1].wait()
    for c in range(6):
        w_ref[0, c] = right[c]

    def precondition(k):
        vector = [w_ref[k, c] for c in range(6)]
        result = []
        for a in range(6):
            if k == 0:
                loads[3 + a].wait()
            total = blocks[6 * a] * vector[0]
            for b in range(1, 6):
                total = total + blocks[6 * a + b] * vector[b]
            result.append(total)
        return result

    flying = []
    gram_rows = {}

    def product(i, j):
        total = None
        for c in range(6):
            term = w_ref[i, c] * w_ref[j, c]
            total = term if total is None else total + term
        total = total[:, 0:128] + total[:, 128:256]
        gram_rows[(i, j)] = jnp.sum(total, axis=0, keepdims=True)

    for k in range(ITERS):
        t = precondition(k)
        pack(k, t)
        tor_moves, pol_moves = tor_copies(k), pol_copies(k)
        if k == 0:

            @pl.when(jnp.logical_not(is_leader))
            def _():
                pl.semaphore_wait(barrier, 4 + 1)

        for copy in pol_moves + tor_moves:
            copy.start()
        if k == 0:
            state_moves = pol_copies(3) + tor_copies(3)
            for copy in state_moves:
                copy.start()
            flying += state_moves
        flying += pol_moves + tor_moves
        for c in range(6):
            t_ref[k, c] = t[c]
        if k == 0:
            loads[2].wait()
        eta = resist[...]
        p = [plasma[c] for c in range(6)]
        f = flux(p, t, 2)
        partial = []
        for c in range(6):
            coefficient = eta if c < 3 else viscosity
            total = inverse_step * t[c] + coefficient * (6.0 * t[c] - up_depth(t[c]) - down_depth(t[c]))
            if f[c] is not None:
                half_flux = 0.5 * f[c]
                total = total + (up_depth(half_flux) - down_depth(half_flux))
            partial.append(total)
        for i in range(k + 1):
            product(i, k)
        if k == 0:
            for copy in state_moves:
                copy.wait_recv()
            for c in range(6):
                up_ref[c] = up_row(plasma[c], pol_rx[3, 1, c : c + 1, :])
                down_ref[c] = down_row(plasma[c], pol_rx[3, 0, c : c + 1, :])
        for copy in pol_moves:
            copy.wait_recv()
        t_up = [
            up_row(t[c], jnp.where(pol == pols - 1, 0.0, pol_rx[k, 1, c : c + 1, :])) for c in range(6)
        ]
        t_down = [down_row(t[c], jnp.where(pol == 0, 0.0, pol_rx[k, 0, c : c + 1, :])) for c in range(6)]
        f_up = flux([up_ref[c] for c in range(6)], t_up, 1)
        f_down = flux([down_ref[c] for c in range(6)], t_down, 1)
        for c in range(6):
            coefficient = eta if c < 3 else viscosity
            partial[c] = partial[c] - coefficient * (t_up[c] + t_down[c])
            if f_up[c] is not None:
                partial[c] = partial[c] + 0.5 * (f_up[c] - f_down[c])
        for copy in tor_moves:
            copy.wait_recv()
        t_up, t_down = from_tor(k, 1), from_tor(k, 0)
        f_up = flux(from_tor(3, 1), t_up, 0)
        f_down = flux(from_tor(3, 0), t_down, 0)
        for c in range(6):
            coefficient = eta if c < 3 else viscosity
            total = partial[c] - coefficient * (t_up[c] + t_down[c])
            if f_up[c] is not None:
                total = total + 0.5 * (f_up[c] - f_down[c])
            w_ref[k + 1, c] = total

    for i in range(ITERS + 1):
        product(i, ITERS)

    wide_lane = lax.broadcasted_iota(jnp.int32, (16, 128), 1)
    wide_sub = lax.broadcasted_iota(jnp.int32, (16, 128), 0)
    rows = jnp.zeros((16, 128), F32)
    for index, pair in enumerate(PAIRS):
        rows = jnp.where(wide_sub == index, jnp.broadcast_to(gram_rows[pair], (16, 128)), rows)
    rows = jnp.broadcast_to(jnp.sum(rows, axis=1, keepdims=True), (16, 128))
    mine = jnp.sum(jnp.where(wide_lane == wide_sub, rows, 0.0), axis=0, keepdims=True)

    def tree(values):
        while len(values) > 1:
            values = [a + b for a, b in zip(values[0::2], values[1::2])]
        return values[0]

    def to_member(index):
        return pltpu.make_async_remote_copy(
            src_ref=sum_ref,
            dst_ref=back_ref,
            send_sem=back_send.at[index],
            recv_sem=back_recv,
            device_id=member_at(index),
            device_id_type=MESH,
        )

    place = leader * members + member
    slot = (place // 8, pl.ds(lax.rem(place, 8), 1))

    def to_root(index):
        return pltpu.make_async_remote_copy(
            src_ref=mine_ref,
            dst_ref=all_sums.at[slot[0], slot[1]],
            send_sem=root_send.at[index],
            recv_sem=root_recv,
            device_id={"tor": index // columns, "pol": (index % columns) * GROUP + 1},
            device_id_type=MESH,
        )

    own = pltpu.make_async_copy(mine_ref, all_sums.at[slot[0], slot[1]], root_recv)
    order = sorted(range(leaders), key=lambda r: r // columns + r % columns)

    def solve(total):
        row_lane = lax.broadcasted_iota(jnp.int32, (1, 128), 1)
        gram = [[None] * (ITERS + 1) for _ in range(ITERS + 1)]
        for index, (i, j) in enumerate(PAIRS):
            entry = jnp.sum(jnp.where(row_lane == index, total, 0.0), axis=1, keepdims=True)
            entry = jnp.broadcast_to(entry, (1, 128))
            gram[i][j] = entry
            gram[j][i] = entry
        alphas, estimates = small_solve(gram, gram[0][0])
        est = jnp.zeros((1, 128), F32)
        for index in range(ITERS):
            est = jnp.where(row_lane == index, estimates[index] * scale, est)
        for index in range(ITERS):
            weights_ref[index : index + 1, :] = alphas[index]
        weights_ref[ITERS : ITERS + 1, :] = est

    mine_ref[...] = mine

    @pl.when(jnp.logical_not(is_leader))
    def _():
        for index in order:
            to_root(index).start()
        for copy in flying:
            copy.wait_send()
        for index in order:
            to_root(index).wait_send()
        to_member(0).wait_recv()
        solve(back_ref[...])

    @pl.when(is_leader)
    def _():
        own.start()
        for index in order:

            @pl.when(leader != index)
            def _():
                to_root(index).start()

        for copy in flying:
            copy.wait_send()
        for index in order:

            @pl.when(leader != index)
            def _():
                to_root(index).wait_send()

        pltpu.make_async_copy(all_sums, all_sums, root_recv).wait()
        total = tree([all_sums[m] for m in range(tors * pols // 8)])
        total = jnp.sum(total, axis=0, keepdims=True)
        sum_ref[...] = total
        backs = [to_member(index) for index in others]
        for copy in backs:
            copy.start()
        solve(total)
        for copy in backs:
            copy.wait_send()


def combine(t_ref, weights_ref, update_ref, est_ref):
    est_ref[...] = weights_ref[ITERS, 0:ITERS]
    full = []
    for k in range(ITERS):
        alpha = weights_ref[k : k + 1, :]
        full.append(jnp.broadcast_to(jnp.concatenate([alpha, alpha], axis=1), (8, 256)))
    for c in range(6):
        update_ref[c] = full[0] * t_ref[0, c] + full[1] * t_ref[1, c] + full[2] * t_ref[2, c]


def solution(mesh):
    sizes = (mesh.shape["tor"], mesh.shape["pol"])

    def shards(plasma_state, right_side, resistivity, jacobi_blocks):
        scale = 1.0 / float(plasma_state.size * sizes[0] * sizes[1]) ** 0.5
        hbm = pl.BlockSpec(memory_space=pl.ANY)
        vmem = pl.BlockSpec(memory_space=pltpu.VMEM)
        tangents, weights = pl.pallas_call(
            functools.partial(kernel, sizes, scale),
            out_shape=(pltpu.VMEM((ITERS, 6, 8, 256), F32), pltpu.VMEM((ITERS + 1, 128), F32)),
            in_specs=[hbm] * 4,
            out_specs=(vmem, vmem),
            scratch_shapes=[
                pltpu.VMEM((6, 8, 256), F32),
                pltpu.VMEM((6, 8, 256), F32),
                pltpu.VMEM((8, 256), F32),
                pltpu.VMEM((36, 8, 256), F32),
                pltpu.VMEM((ITERS + 1, 6, 8, 256), F32),
                pltpu.VMEM((6, 8, 256), F32),
                pltpu.VMEM((6, 8, 256), F32),
                pltpu.VMEM((4, 48, 256), BF16),
                pltpu.VMEM((4, 2, 48, 256), BF16),
                pltpu.VMEM((4, 2, 6, 256), F32),
                pltpu.VMEM((4, 2, 6, 256), F32),
                pltpu.VMEM((1, 128), F32),
                pltpu.VMEM((1, 128), F32),
                pltpu.VMEM((1, 128), F32),
                pltpu.VMEM((64, 8, 128), F32),
                pltpu.SemaphoreType.DMA((9,)),
                pltpu.SemaphoreType.DMA((4, 2)),
                pltpu.SemaphoreType.DMA((4, 2)),
                pltpu.SemaphoreType.DMA((4, 2)),
                pltpu.SemaphoreType.DMA((4, 2)),
                pltpu.SemaphoreType.DMA((32,)),
                pltpu.SemaphoreType.DMA,
                pltpu.SemaphoreType.DMA((16,)),
                pltpu.SemaphoreType.DMA,
            ],
            compiler_params=pltpu.CompilerParams(collective_id=0, has_side_effects=True),
            name="krylov",
        )(
            plasma_state.reshape(6, 8, 256),
            right_side.reshape(6, 8, 256),
            resistivity.reshape(8, 256),
            jacobi_blocks.reshape(36, 8, 256),
        )
        update, est = pl.pallas_call(
            combine,
            out_shape=(jax.ShapeDtypeStruct((6, 8, 256), F32), jax.ShapeDtypeStruct((ITERS,), F32)),
            in_specs=[vmem] * 2,
            out_specs=(vmem, vmem),
            name="combine",
        )(
            pltpu.with_memory_space_constraint(tangents, pltpu.VMEM),
            pltpu.with_memory_space_constraint(weights, pltpu.VMEM),
        )
        return update.reshape(6, 1, 8, 256), est

    return jax.shard_map(
        shards,
        mesh=mesh,
        in_specs=(
            P(None, "tor", "pol", None),
            P(None, "tor", "pol", None),
            P("tor", "pol", None),
            P(None, None, "tor", "pol", None),
        ),
        out_specs=(P(None, "tor", "pol", None), P()),
        check_vma=False,
    )
```

```python
import functools

import jax
import jax.numpy as jnp
from jax import lax
from jax.experimental import pallas as pl
from jax.experimental.pallas import tpu as pltpu
from jax.sharding import PartitionSpec as P

ITERS = 3
inverse_step = 1.0
viscosity = 0.2
epsilon = 1e-06

MESH = pl.DeviceIdType.MESH
F32 = jnp.float32
BF16 = jnp.bfloat16
PAIRS = [(i, j) for j in range(ITERS + 1) for i in range(j + 1)]
GROUP = 8


def flux(p, t, k):
    B, V, b, w = p[0:3], p[3:6], t[0:3], t[3:6]
    parts = []
    for i in range(3):
        parts.append(None if i == k else w[k] * B[i] + V[k] * b[i] - b[k] * V[i] - B[k] * w[i])
    for i in range(3):
        moment = w[k] * V[i] + V[k] * w[i] - b[k] * B[i] - B[k] * b[i]
        if i == k:
            moment = moment + (B[0] * b[0] + B[1] * b[1] + B[2] * b[2])
        parts.append(moment)
    return parts


def small_solve(gram, like):
    count = ITERS
    zero = jnp.zeros_like(like)
    norm0 = jnp.sqrt(gram[0][0] + epsilon)
    coefs = [[1.0 / norm0]]
    columns = []
    for j in range(count):
        shifted = [None] + coefs[j]
        size = j + 2
        applied = []
        for row in range(size):
            total = None
            for col in range(1, size):
                term = gram[row][col] * shifted[col]
                total = term if total is None else total + term
            applied.append(total)
        column = []
        for i in range(j + 1):
            total = None
            for row in range(i + 1):
                term = coefs[i][row] * applied[row]
                total = term if total is None else total + term
            column.append(total)
        remainder = []
        for row in range(size):
            total = shifted[row]
            for i in range(j + 1):
                if row <= i:
                    term = column[i] * coefs[i][row]
                    total = -term if total is None else total - term
            remainder.append(total)
        square = None
        for row in range(size):
            inner = None
            for col in range(size):
                term = gram[row][col] * remainder[col]
                inner = term if inner is None else inner + term
            term = inner * remainder[row]
            square = term if square is None else square + term
        norm = jnp.sqrt(jnp.maximum(square, 0.0) + epsilon)
        columns.append(column + [norm])
        if j + 1 < count:
            inverse = 1.0 / norm
            coefs.append([entry * inverse for entry in remainder])
    rhs = [norm0] + [zero] * count
    cosines, sines, triangle, estimates = [], [], [], []
    for column in range(count):
        entries = list(columns[column])
        for i in range(column):
            first, second = entries[i], entries[i + 1]
            entries[i] = cosines[i] * first + sines[i] * second
            entries[i + 1] = cosines[i] * second - sines[i] * first
        first, second = entries[column], entries[column + 1]
        radius = jnp.sqrt(first * first + second * second)
        inverse = 1.0 / radius
        cosine, sine = first * inverse, second * inverse
        cosines.append(cosine)
        sines.append(sine)
        triangle.append(entries[:column] + [inverse])
        previous = rhs[column]
        rhs[column] = cosine * previous
        rhs[column + 1] = -sine * previous
        estimates.append(jnp.abs(rhs[column + 1]))
    weights = [zero] * count
    for column in reversed(range(count)):
        value = rhs[column]
        for later in range(column + 1, count):
            value = value - triangle[later][column] * weights[later]
        weights[column] = value * triangle[column][column]
    alphas = []
    for row in range(count):
        total = None
        for j in range(row, count):
            term = weights[j] * coefs[j][row]
            total = term if total is None else total + term
        alphas.append(total)
    return alphas, estimates


def kernel(sizes, scale, plasma_hbm, right_hbm, resist_hbm, blocks_hbm, t_ref, weights_ref,
           plasma, right, resist, blocks, w_ref, up_ref, down_ref,
           tor_tx, tor_rx, pol_tx, pol_rx, mine_ref, back_ref, sum_ref, all_sums,
           load_sem, tor_send, tor_recv, pol_send, pol_recv,
           root_send, root_recv, back_send, back_recv):
    tors, pols = sizes
    halves = 2
    width = tors // halves
    columns = pols // GROUP
    members = halves * GROUP
    leaders = width * columns
    tor = lax.axis_index("tor")
    pol = lax.axis_index("pol")
    tor_next, tor_prev = lax.rem(tor + 1, tors), lax.rem(tor + tors - 1, tors)
    pol_next, pol_prev = lax.rem(pol + 1, pols), lax.rem(pol + pols - 1, pols)

    half, lead_tor = tor // width, lax.rem(tor, width)
    column, inner = pol // GROUP, lax.rem(pol, GROUP)
    member = half * GROUP + inner
    leader = lead_tor * columns + column
    roots = leaders + 1
    root = tor * columns + column
    is_root = jnp.logical_and(inner == 1, root < roots)

    def member_at(index):
        return {"tor": (index // GROUP) * width + lead_tor, "pol": column * GROUP + index % GROUP}

    def root_at(index):
        return {"tor": index // columns, "pol": lax.rem(index, columns) * GROUP + 1}

    def for_members(act):
        @pl.when(root != 0)
        def _():
            for index in range(members):
                if index not in (1, GROUP + 1):
                    act(index)

        @pl.when(jnp.logical_and(root != 0, root != leaders))
        def _():
            act(GROUP + 1)


    barrier = pltpu.get_barrier_semaphore()
    for neighbour in (pol_next, pol_prev):
        pl.semaphore_signal(barrier, inc=1, device_id={"tor": tor, "pol": neighbour}, device_id_type=MESH)
    for neighbour in (tor_next, tor_prev):
        pl.semaphore_signal(barrier, inc=1, device_id={"tor": neighbour, "pol": pol}, device_id_type=MESH)

    loads = [
        pltpu.make_async_copy(plasma_hbm, plasma, load_sem.at[0]),
        pltpu.make_async_copy(right_hbm, right, load_sem.at[1]),
        pltpu.make_async_copy(resist_hbm, resist, load_sem.at[2]),
    ]
    for row in range(6):
        loads.append(
            pltpu.make_async_copy(
                blocks_hbm.at[pl.ds(6 * row, 6)], blocks.at[pl.ds(6 * row, 6)], load_sem.at[3 + row]
            )
        )
    for load in loads:
        load.start()

    @pl.when(is_root)
    def _():
        for step in range(1, roots):
            partner = root_at(lax.rem(root + step, roots))
            pl.semaphore_signal(barrier, inc=1, device_id=partner, device_id_type=MESH)
        pl.semaphore_wait(barrier, 4 + roots - 1)
        for_members(
            lambda index: pl.semaphore_signal(barrier, inc=1, device_id=member_at(index), device_id_type=MESH)
        )

    lane = lax.broadcasted_iota(jnp.int32, (8, 256), 1)
    sub = lax.broadcasted_iota(jnp.int32, (8, 256), 0)

    def up_depth(x):
        return jnp.where(lane == 255, 0.0, pltpu.roll(x, 255, 1))

    def down_depth(x):
        return jnp.where(lane == 0, 0.0, pltpu.roll(x, 1, 1))

    def up_row(x, halo):
        return jnp.where(sub == 7, jnp.broadcast_to(halo, (8, 256)), pltpu.roll(x, 7, 0))

    def down_row(x, halo):
        return jnp.where(sub == 0, jnp.broadcast_to(halo, (8, 256)), pltpu.roll(x, 1, 0))

    def tor_copies(slot):
        return [
            pltpu.make_async_remote_copy(
                src_ref=tor_tx.at[slot],
                dst_ref=tor_rx.at[slot, way],
                send_sem=tor_send.at[slot, way],
                recv_sem=tor_recv.at[slot, way],
                device_id={"tor": (tor_next, tor_prev)[way], "pol": pol},
                device_id_type=MESH,
            )
            for way in range(2)
        ]

    def pol_copies(slot):
        return [
            pltpu.make_async_remote_copy(
                src_ref=pol_tx.at[slot, way],
                dst_ref=pol_rx.at[slot, way],
                send_sem=pol_send.at[slot, way],
                recv_sem=pol_recv.at[slot, way],
                device_id={"tor": tor, "pol": (pol_next, pol_prev)[way]},
                device_id_type=MESH,
            )
            for way in range(2)
        ]

    def pack_tor(slot, x):
        for pair in range(3):
            tor_tx[slot, 16 * pair : 16 * pair + 16, :] = jnp.concatenate(
                [x[2 * pair], x[2 * pair + 1]], axis=0
            ).astype(BF16)

    def pack_pol(slot, x):
        for c in range(6):
            pol_tx[slot, 0, c : c + 1, :] = x[c][7:8, :]
            pol_tx[slot, 1, c : c + 1, :] = x[c][0:1, :]

    def from_tor(slot, way):
        planes = []
        for pair in range(3):
            both = tor_rx[slot, way, 16 * pair : 16 * pair + 16, :].astype(F32)
            planes += [both[0:8], both[8:16]]
        return planes

    loads[0].wait()
    pack_tor(3, [plasma[c] for c in range(6)])
    pack_pol(3, [plasma[c] for c in range(6)])
    loads[1].wait()
    for c in range(6):
        w_ref[0, c] = right[c]

    def precondition(k):
        vector = [w_ref[k, c] for c in range(6)]
        result = []
        for a in range(6):
            if k == 0:
                loads[3 + a].wait()
            total = blocks[6 * a] * vector[0]
            for b in range(1, 6):
                total = total + blocks[6 * a + b] * vector[b]
            result.append(total)
        return result

    flying = []
    gram_rows = {}

    def product(i, j):
        total = None
        for c in range(6):
            term = w_ref[i, c] * w_ref[j, c]
            total = term if total is None else total + term
        total = total[:, 0:128] + total[:, 128:256]
        gram_rows[(i, j)] = jnp.sum(total, axis=0, keepdims=True)

    for k in range(ITERS):
        t = precondition(k)
        pack_tor(k, t)
        tor_moves, pol_moves = tor_copies(k), pol_copies(k)
        if k == 0:

            @pl.when(jnp.logical_not(is_root))
            def _():
                pl.semaphore_wait(barrier, 4 + 1)

        for copy in tor_moves:
            copy.start()
        pack_pol(k, t)
        for copy in pol_moves:
            copy.start()
        if k == 0:
            state_moves = tor_copies(3) + pol_copies(3)
            for copy in state_moves:
                copy.start()
            flying += state_moves
        flying += pol_moves + tor_moves
        for c in range(6):
            t_ref[k, c] = t[c]
        if k == 0:
            loads[2].wait()
        eta = resist[...]
        p = [plasma[c] for c in range(6)]
        f = flux(p, t, 2)
        partial = []
        for c in range(6):
            coefficient = eta if c < 3 else viscosity
            total = inverse_step * t[c] + coefficient * (6.0 * t[c] - up_depth(t[c]) - down_depth(t[c]))
            if f[c] is not None:
                half_flux = 0.5 * f[c]
                total = total + (up_depth(half_flux) - down_depth(half_flux))
            partial.append(total)
        for i in range(k + 1):
            product(i, k)
        if k == 0:
            for copy in state_moves:
                copy.wait_recv()
            for c in range(6):
                up_ref[c] = up_row(plasma[c], pol_rx[3, 1, c : c + 1, :])
                down_ref[c] = down_row(plasma[c], pol_rx[3, 0, c : c + 1, :])
        for copy in pol_moves:
            copy.wait_recv()
        t_up = [
            up_row(t[c], jnp.where(pol == pols - 1, 0.0, pol_rx[k, 1, c : c + 1, :])) for c in range(6)
        ]
        t_down = [down_row(t[c], jnp.where(pol == 0, 0.0, pol_rx[k, 0, c : c + 1, :])) for c in range(6)]
        f_up = flux([up_ref[c] for c in range(6)], t_up, 1)
        f_down = flux([down_ref[c] for c in range(6)], t_down, 1)
        for c in range(6):
            coefficient = eta if c < 3 else viscosity
            partial[c] = partial[c] - coefficient * (t_up[c] + t_down[c])
            if f_up[c] is not None:
                partial[c] = partial[c] + 0.5 * (f_up[c] - f_down[c])
        for copy in tor_moves:
            copy.wait_recv()
        t_up, t_down = from_tor(k, 1), from_tor(k, 0)
        f_up = flux(from_tor(3, 1), t_up, 0)
        f_down = flux(from_tor(3, 0), t_down, 0)
        for c in range(6):
            coefficient = eta if c < 3 else viscosity
            total = partial[c] - coefficient * (t_up[c] + t_down[c])
            if f_up[c] is not None:
                total = total + 0.5 * (f_up[c] - f_down[c])
            w_ref[k + 1, c] = total

    for i in range(ITERS + 1):
        product(i, ITERS)

    wide_lane = lax.broadcasted_iota(jnp.int32, (16, 128), 1)
    wide_sub = lax.broadcasted_iota(jnp.int32, (16, 128), 0)
    rows = jnp.zeros((16, 128), F32)
    for index, pair in enumerate(PAIRS):
        rows = jnp.where(wide_sub == index, jnp.broadcast_to(gram_rows[pair], (16, 128)), rows)
    rows = jnp.broadcast_to(jnp.sum(rows, axis=1, keepdims=True), (16, 128))
    mine = jnp.sum(jnp.where(wide_lane == wide_sub, rows, 0.0), axis=0, keepdims=True)

    def tree(values):
        while len(values) > 1:
            values = [a + b for a, b in zip(values[0::2], values[1::2])]
        return values[0]

    def to_member(index):
        return pltpu.make_async_remote_copy(
            src_ref=sum_ref,
            dst_ref=back_ref,
            send_sem=back_send.at[index],
            recv_sem=back_recv,
            device_id=member_at(index),
            device_id_type=MESH,
        )

    place = leader * members + member
    slot = (place // 8, pl.ds(lax.rem(place, 8), 1))

    def to_root(index):
        return pltpu.make_async_remote_copy(
            src_ref=mine_ref,
            dst_ref=all_sums.at[slot[0], slot[1]],
            send_sem=root_send.at[index],
            recv_sem=root_recv,
            device_id={"tor": index // columns, "pol": (index % columns) * GROUP + 1},
            device_id_type=MESH,
        )

    own = pltpu.make_async_copy(mine_ref, all_sums.at[slot[0], slot[1]], root_recv)
    order = sorted(range(roots), key=lambda r: r // columns + r % columns)

    def solve(total):
        row_lane = lax.broadcasted_iota(jnp.int32, (1, 128), 1)
        gram = [[None] * (ITERS + 1) for _ in range(ITERS + 1)]
        for index, (i, j) in enumerate(PAIRS):
            entry = jnp.sum(jnp.where(row_lane == index, total, 0.0), axis=1, keepdims=True)
            entry = jnp.broadcast_to(entry, (1, 128))
            gram[i][j] = entry
            gram[j][i] = entry
        alphas, estimates = small_solve(gram, gram[0][0])
        est = jnp.zeros((1, 128), F32)
        for index in range(ITERS):
            est = jnp.where(row_lane == index, estimates[index] * scale, est)
        for index in range(ITERS):
            weights_ref[index : index + 1, :] = alphas[index]
        weights_ref[ITERS : ITERS + 1, :] = est

    mine_ref[...] = mine

    @pl.when(jnp.logical_not(is_root))
    def _():
        for index in order:
            to_root(index).start()
        for copy in flying:
            copy.wait_send()
        for index in order:
            to_root(index).wait_send()
        to_member(0).wait_recv()
        solve(back_ref[...])

    @pl.when(is_root)
    def _():
        own.start()
        for index in order:

            @pl.when(root != index)
            def _():
                to_root(index).start()

        for copy in flying:
            copy.wait_send()
        for index in order:

            @pl.when(root != index)
            def _():
                to_root(index).wait_send()

        pltpu.make_async_copy(all_sums, all_sums, root_recv).wait()
        total = tree([all_sums[m] for m in range(tors * pols // 8)])
        total = jnp.sum(total, axis=0, keepdims=True)
        sum_ref[...] = total
        for_members(lambda index: to_member(index).start())
        solve(total)
        for_members(lambda index: to_member(index).wait_send())


def combine(t_ref, weights_ref, update_ref, est_ref):
    est_ref[...] = weights_ref[ITERS, 0:ITERS]
    full = []
    for k in range(ITERS):
        alpha = weights_ref[k : k + 1, :]
        full.append(jnp.broadcast_to(jnp.concatenate([alpha, alpha], axis=1), (8, 256)))
    for c in range(6):
        update_ref[c] = full[0] * t_ref[0, c] + full[1] * t_ref[1, c] + full[2] * t_ref[2, c]


def solution(mesh):
    sizes = (mesh.shape["tor"], mesh.shape["pol"])

    def shards(plasma_state, right_side, resistivity, jacobi_blocks):
        scale = 1.0 / float(plasma_state.size * sizes[0] * sizes[1]) ** 0.5
        hbm = pl.BlockSpec(memory_space=pl.ANY)
        vmem = pl.BlockSpec(memory_space=pltpu.VMEM)
        tangents, weights = pl.pallas_call(
            functools.partial(kernel, sizes, scale),
            out_shape=(pltpu.VMEM((ITERS, 6, 8, 256), F32), pltpu.VMEM((ITERS + 1, 128), F32)),
            in_specs=[hbm] * 4,
            out_specs=(vmem, vmem),
            scratch_shapes=[
                pltpu.VMEM((6, 8, 256), F32),
                pltpu.VMEM((6, 8, 256), F32),
                pltpu.VMEM((8, 256), F32),
                pltpu.VMEM((36, 8, 256), F32),
                pltpu.VMEM((ITERS + 1, 6, 8, 256), F32),
                pltpu.VMEM((6, 8, 256), F32),
                pltpu.VMEM((6, 8, 256), F32),
                pltpu.VMEM((4, 48, 256), BF16),
                pltpu.VMEM((4, 2, 48, 256), BF16),
                pltpu.VMEM((4, 2, 6, 256), F32),
                pltpu.VMEM((4, 2, 6, 256), F32),
                pltpu.VMEM((1, 128), F32),
                pltpu.VMEM((1, 128), F32),
                pltpu.VMEM((1, 128), F32),
                pltpu.VMEM((64, 8, 128), F32),
                pltpu.SemaphoreType.DMA((9,)),
                pltpu.SemaphoreType.DMA((4, 2)),
                pltpu.SemaphoreType.DMA((4, 2)),
                pltpu.SemaphoreType.DMA((4, 2)),
                pltpu.SemaphoreType.DMA((4, 2)),
                pltpu.SemaphoreType.DMA((33,)),
                pltpu.SemaphoreType.DMA,
                pltpu.SemaphoreType.DMA((16,)),
                pltpu.SemaphoreType.DMA,
            ],
            compiler_params=pltpu.CompilerParams(collective_id=0, has_side_effects=True),
            name="krylov",
        )(
            plasma_state.reshape(6, 8, 256),
            right_side.reshape(6, 8, 256),
            resistivity.reshape(8, 256),
            jacobi_blocks.reshape(36, 8, 256),
        )
        update, est = pl.pallas_call(
            combine,
            out_shape=(jax.ShapeDtypeStruct((6, 8, 256), F32), jax.ShapeDtypeStruct((ITERS,), F32)),
            in_specs=[vmem] * 2,
            out_specs=(vmem, vmem),
            name="combine",
        )(
            pltpu.with_memory_space_constraint(tangents, pltpu.VMEM),
            pltpu.with_memory_space_constraint(weights, pltpu.VMEM),
        )
        return update.reshape(6, 1, 8, 256), est

    return jax.shard_map(
        shards,
        mesh=mesh,
        in_specs=(
            P(None, "tor", "pol", None),
            P(None, "tor", "pol", None),
            P("tor", "pol", None),
            P(None, None, "tor", "pol", None),
        ),
        out_specs=(P(None, "tor", "pol", None), P()),
        check_vma=False,
    )
```

```python
import functools

import jax
import jax.numpy as jnp
from jax import lax
from jax.experimental import pallas as pl
from jax.experimental.pallas import tpu as pltpu
from jax.sharding import PartitionSpec as P

ITERS = 3
inverse_step = 1.0
viscosity = 0.2
epsilon = 1e-06

MESH = pl.DeviceIdType.MESH
F32 = jnp.float32
BF16 = jnp.bfloat16
PAIRS = [(i, j) for j in range(ITERS + 1) for i in range(j + 1)]
GROUP = 8


def flux(p, t, k):
    B, V, b, w = p[0:3], p[3:6], t[0:3], t[3:6]
    parts = []
    for i in range(3):
        parts.append(None if i == k else w[k] * B[i] + V[k] * b[i] - b[k] * V[i] - B[k] * w[i])
    for i in range(3):
        moment = w[k] * V[i] + V[k] * w[i] - b[k] * B[i] - B[k] * b[i]
        if i == k:
            moment = moment + (B[0] * b[0] + B[1] * b[1] + B[2] * b[2])
        parts.append(moment)
    return parts


def small_solve(gram, like):
    count = ITERS
    zero = jnp.zeros_like(like)
    norm0 = jnp.sqrt(gram[0][0] + epsilon)
    coefs = [[1.0 / norm0]]
    columns = []
    for j in range(count):
        shifted = [None] + coefs[j]
        size = j + 2
        applied = []
        for row in range(size):
            total = None
            for col in range(1, size):
                term = gram[row][col] * shifted[col]
                total = term if total is None else total + term
            applied.append(total)
        column = []
        for i in range(j + 1):
            total = None
            for row in range(i + 1):
                term = coefs[i][row] * applied[row]
                total = term if total is None else total + term
            column.append(total)
        remainder = []
        for row in range(size):
            total = shifted[row]
            for i in range(j + 1):
                if row <= i:
                    term = column[i] * coefs[i][row]
                    total = -term if total is None else total - term
            remainder.append(total)
        square = None
        for row in range(size):
            inner = None
            for col in range(size):
                term = gram[row][col] * remainder[col]
                inner = term if inner is None else inner + term
            term = inner * remainder[row]
            square = term if square is None else square + term
        norm = jnp.sqrt(jnp.maximum(square, 0.0) + epsilon)
        columns.append(column + [norm])
        if j + 1 < count:
            inverse = 1.0 / norm
            coefs.append([entry * inverse for entry in remainder])
    rhs = [norm0] + [zero] * count
    cosines, sines, triangle, estimates = [], [], [], []
    for column in range(count):
        entries = list(columns[column])
        for i in range(column):
            first, second = entries[i], entries[i + 1]
            entries[i] = cosines[i] * first + sines[i] * second
            entries[i + 1] = cosines[i] * second - sines[i] * first
        first, second = entries[column], entries[column + 1]
        radius = jnp.sqrt(first * first + second * second)
        inverse = 1.0 / radius
        cosine, sine = first * inverse, second * inverse
        cosines.append(cosine)
        sines.append(sine)
        triangle.append(entries[:column] + [inverse])
        previous = rhs[column]
        rhs[column] = cosine * previous
        rhs[column + 1] = -sine * previous
        estimates.append(jnp.abs(rhs[column + 1]))
    weights = [zero] * count
    for column in reversed(range(count)):
        value = rhs[column]
        for later in range(column + 1, count):
            value = value - triangle[later][column] * weights[later]
        weights[column] = value * triangle[column][column]
    alphas = []
    for row in range(count):
        total = None
        for j in range(row, count):
            term = weights[j] * coefs[j][row]
            total = term if total is None else total + term
        alphas.append(total)
    return alphas, estimates


def kernel(sizes, scale, plasma_hbm, right_hbm, resist_hbm, blocks_hbm, t_ref, weights_ref,
           plasma, right, resist, blocks, w_ref, up_ref, down_ref,
           tor_tx, tor_rx, pol_tx, pol_rx, mix_tx, mix_rx, edge_tx, edge_rx, mine_ref, back_ref, sum_ref, all_sums,
           load_sem, tor_send, tor_recv, pol_send, pol_recv,
           root_send, root_recv, back_send, back_recv):
    tors, pols = sizes
    halves = 2
    width = tors // halves
    columns = pols // GROUP
    members = halves * GROUP
    leaders = width * columns
    tor = lax.axis_index("tor")
    pol = lax.axis_index("pol")
    tor_next, tor_prev = lax.rem(tor + 1, tors), lax.rem(tor + tors - 1, tors)
    pol_next, pol_prev = lax.rem(pol + 1, pols), lax.rem(pol + pols - 1, pols)

    half, lead_tor = tor // width, lax.rem(tor, width)
    column, inner = pol // GROUP, lax.rem(pol, GROUP)
    member = half * GROUP + inner
    leader = lead_tor * columns + column
    roots = leaders + 1
    root = tor * columns + column
    is_root = jnp.logical_and(inner == 1, root < roots)

    def member_at(index):
        return {"tor": (index // GROUP) * width + lead_tor, "pol": column * GROUP + index % GROUP}

    def root_at(index):
        return {"tor": index // columns, "pol": lax.rem(index, columns) * GROUP + 1}

    def for_members(act):
        @pl.when(root != 0)
        def _():
            for index in range(members):
                if index not in (1, GROUP + 1):
                    act(index)

        @pl.when(jnp.logical_and(root != 0, root != leaders))
        def _():
            act(GROUP + 1)


    barrier = pltpu.get_barrier_semaphore()
    for neighbour in (tor_next, tor_prev):
        pl.semaphore_signal(barrier, inc=1, device_id={"tor": neighbour, "pol": pol}, device_id_type=MESH)
    for neighbour in (pol_next, pol_prev):
        pl.semaphore_signal(barrier, inc=1, device_id={"tor": tor, "pol": neighbour}, device_id_type=MESH)

    loads = [
        pltpu.make_async_copy(plasma_hbm, plasma, load_sem.at[0]),
        pltpu.make_async_copy(right_hbm, right, load_sem.at[1]),
        pltpu.make_async_copy(resist_hbm, resist, load_sem.at[2]),
    ]
    for row in range(6):
        loads.append(
            pltpu.make_async_copy(
                blocks_hbm.at[pl.ds(6 * row, 6)], blocks.at[pl.ds(6 * row, 6)], load_sem.at[3 + row]
            )
        )
    for load in loads:
        load.start()

    @pl.when(is_root)
    def _():
        for step in range(1, roots):
            partner = root_at(lax.rem(root + step, roots))
            pl.semaphore_signal(barrier, inc=1, device_id=partner, device_id_type=MESH)
        pl.semaphore_wait(barrier, 4 + roots - 1)
        for_members(
            lambda index: pl.semaphore_signal(barrier, inc=1, device_id=member_at(index), device_id_type=MESH)
        )

    lane = lax.broadcasted_iota(jnp.int32, (8, 256), 1)
    sub = lax.broadcasted_iota(jnp.int32, (8, 256), 0)

    def up_depth(x):
        return jnp.where(lane == 255, 0.0, pltpu.roll(x, 255, 1))

    def down_depth(x):
        return jnp.where(lane == 0, 0.0, pltpu.roll(x, 1, 1))

    def up_row(x, halo):
        return jnp.where(sub == 7, jnp.broadcast_to(halo, (8, 256)), pltpu.roll(x, 7, 0))

    def down_row(x, halo):
        return jnp.where(sub == 0, jnp.broadcast_to(halo, (8, 256)), pltpu.roll(x, 1, 0))

    def tor_copies(slot):
        return [
            pltpu.make_async_remote_copy(
                src_ref=tor_tx.at[slot],
                dst_ref=tor_rx.at[slot, way],
                send_sem=tor_send.at[slot, way],
                recv_sem=tor_recv.at[slot, way],
                device_id={"tor": (tor_next, tor_prev)[way], "pol": pol},
                device_id_type=MESH,
            )
            for way in range(2)
        ]

    def pol_copies(slot):
        return [
            pltpu.make_async_remote_copy(
                src_ref=pol_tx.at[slot, way],
                dst_ref=pol_rx.at[slot, way],
                send_sem=pol_send.at[slot, way],
                recv_sem=pol_recv.at[slot, way],
                device_id={"tor": tor, "pol": (pol_next, pol_prev)[way]},
                device_id_type=MESH,
            )
            for way in range(2)
        ]

    def mixed(t, direction):
        f = flux(own_plasma, t, direction)
        half = [None if f[c] is None else 0.5 * f[c] for c in range(6)]
        planes = []
        for sign in (-1.0, 1.0):
            planes.append(
                [sign * half[c] - viscosity * t[c] for c in (3, 4, 5)]
                + [t[0], t[1], t[2]]
                + [sign * half[c] for c in range(3) if c != direction]
            )
        return planes

    def mixed_copies(tor_way):
        if tor_way:
            src, dst, send, recv = mix_tx, mix_rx, tor_send, tor_recv
        else:
            src, dst, send, recv = edge_tx, edge_rx, pol_send, pol_recv
        return [
            pltpu.make_async_remote_copy(
                src_ref=src.at[way],
                dst_ref=dst.at[way],
                send_sem=send.at[0, way],
                recv_sem=recv.at[0, way],
                device_id=(
                    {"tor": (tor_next, tor_prev)[way], "pol": pol}
                    if tor_way
                    else {"tor": tor, "pol": (pol_next, pol_prev)[way]}
                ),
                device_id_type=MESH,
            )
            for way in range(2)
        ]

    def add_mixed(partial, planes, direction):
        partial = list(partial)
        others = [c for c in range(3) if c != direction]
        for index in range(3):
            partial[3 + index] = partial[3 + index] + planes[index]
            partial[index] = partial[index] - eta * planes[3 + index]
        for index, c in enumerate(others):
            partial[c] = partial[c] + planes[6 + index]
        return partial

    def pack_tor(slot, x):
        for pair in range(3):
            tor_tx[slot, 16 * pair : 16 * pair + 16, :] = jnp.concatenate(
                [x[2 * pair], x[2 * pair + 1]], axis=0
            ).astype(BF16)

    def pack_pol(slot, x):
        for c in range(6):
            pol_tx[slot, 0, c : c + 1, :] = x[c][7:8, :]
            pol_tx[slot, 1, c : c + 1, :] = x[c][0:1, :]

    def from_tor(slot, way):
        planes = []
        for pair in range(3):
            both = tor_rx[slot, way, 16 * pair : 16 * pair + 16, :].astype(F32)
            planes += [both[0:8], both[8:16]]
        return planes

    loads[0].wait()
    own_plasma = [plasma[c] for c in range(6)]
    pack_tor(3, own_plasma)
    pack_pol(3, own_plasma)
    loads[1].wait()
    for c in range(6):
        w_ref[0, c] = right[c]

    def precondition(k):
        vector = [w_ref[k, c] for c in range(6)]
        result = []
        for a in range(6):
            if k == 0:
                loads[3 + a].wait()
            total = blocks[6 * a] * vector[0]
            for b in range(1, 6):
                total = total + blocks[6 * a + b] * vector[b]
            result.append(total)
        return result

    flying = []
    gram_rows = {}

    def product(i, j):
        total = None
        for c in range(6):
            term = w_ref[i, c] * w_ref[j, c]
            total = term if total is None else total + term
        total = total[:, 0:128] + total[:, 128:256]
        gram_rows[(i, j)] = jnp.sum(total, axis=0, keepdims=True)

    def local(t):
        f = flux(own_plasma, t, 2)
        partial = []
        for c in range(6):
            coefficient = eta if c < 3 else viscosity
            total = inverse_step * t[c] + coefficient * (6.0 * t[c] - up_depth(t[c]) - down_depth(t[c]))
            if f[c] is not None:
                half_flux = 0.5 * f[c]
                total = total + (up_depth(half_flux) - down_depth(half_flux))
            partial.append(total)
        return partial

    def outside(way, row):
        return jnp.where(pol == (pols - 1 if way == 1 else 0), 0.0, row)

    t = precondition(0)
    along_tor, along_pol = mixed(t, 0), mixed(t, 1)
    for way in range(2):
        for pair in range(4):
            mix_tx[way, 16 * pair : 16 * pair + 16, :] = jnp.concatenate(
                [along_tor[way][2 * pair], along_tor[way][2 * pair + 1]], axis=0
            ).astype(BF16)
        for index in range(8):
            edge_tx[way, index : index + 1, :] = along_pol[way][index][7 - 7 * way : 8 - 7 * way, :]

    @pl.when(jnp.logical_not(is_root))
    def _():
        pl.semaphore_wait(barrier, 4 + 1)

    tor_moves, pol_moves = mixed_copies(True), mixed_copies(False)
    state_moves = tor_copies(3) + pol_copies(3)
    for copy in tor_moves + pol_moves + state_moves:
        copy.start()
    flying += tor_moves + pol_moves + state_moves
    for c in range(6):
        t_ref[0, c] = t[c]
    loads[2].wait()
    eta = resist[...]
    partial = local(t)
    product(0, 0)
    for copy in pol_moves:
        copy.wait_recv()
    after = [outside(1, edge_rx[1, index : index + 1, :]) for index in range(8)]
    before = [outside(0, edge_rx[0, index : index + 1, :]) for index in range(8)]
    partial = add_mixed(partial, [up_row(along_pol[1][index], after[index]) for index in range(8)], 1)
    partial = add_mixed(partial, [down_row(along_pol[0][index], before[index]) for index in range(8)], 1)
    for copy in tor_moves:
        copy.wait_recv()
    for way in range(2):
        planes = []
        for pair in range(4):
            both = mix_rx[way, 16 * pair : 16 * pair + 16, :].astype(F32)
            planes += [both[0:8], both[8:16]]
        partial = add_mixed(partial, planes, 0)
    for c in range(6):
        w_ref[1, c] = partial[c]

    for k in range(1, ITERS):
        t = precondition(k)
        pack_tor(k, t)
        tor_moves, pol_moves = tor_copies(k), pol_copies(k)
        for copy in tor_moves:
            copy.start()
        pack_pol(k, t)
        for copy in pol_moves:
            copy.start()
        flying += pol_moves + tor_moves
        for c in range(6):
            t_ref[k, c] = t[c]
        partial = local(t)
        for i in range(k + 1):
            product(i, k)
        if k == 1:
            for copy in state_moves:
                copy.wait_recv()
            for c in range(6):
                up_ref[c] = up_row(plasma[c], pol_rx[3, 1, c : c + 1, :])
                down_ref[c] = down_row(plasma[c], pol_rx[3, 0, c : c + 1, :])
        for copy in pol_moves:
            copy.wait_recv()
        t_up = [up_row(t[c], outside(1, pol_rx[k, 1, c : c + 1, :])) for c in range(6)]
        t_down = [down_row(t[c], outside(0, pol_rx[k, 0, c : c + 1, :])) for c in range(6)]
        f_up = flux([up_ref[c] for c in range(6)], t_up, 1)
        f_down = flux([down_ref[c] for c in range(6)], t_down, 1)
        for c in range(6):
            coefficient = eta if c < 3 else viscosity
            partial[c] = partial[c] - coefficient * (t_up[c] + t_down[c])
            if f_up[c] is not None:
                partial[c] = partial[c] + 0.5 * (f_up[c] - f_down[c])
        for copy in tor_moves:
            copy.wait_recv()
        t_up, t_down = from_tor(k, 1), from_tor(k, 0)
        f_up = flux(from_tor(3, 1), t_up, 0)
        f_down = flux(from_tor(3, 0), t_down, 0)
        for c in range(6):
            coefficient = eta if c < 3 else viscosity
            total = partial[c] - coefficient * (t_up[c] + t_down[c])
            if f_up[c] is not None:
                total = total + 0.5 * (f_up[c] - f_down[c])
            w_ref[k + 1, c] = total

    for i in range(ITERS + 1):
        product(i, ITERS)

    wide_lane = lax.broadcasted_iota(jnp.int32, (16, 128), 1)
    wide_sub = lax.broadcasted_iota(jnp.int32, (16, 128), 0)
    rows = jnp.zeros((16, 128), F32)
    for index, pair in enumerate(PAIRS):
        rows = jnp.where(wide_sub == index, jnp.broadcast_to(gram_rows[pair], (16, 128)), rows)
    rows = jnp.broadcast_to(jnp.sum(rows, axis=1, keepdims=True), (16, 128))
    mine = jnp.sum(jnp.where(wide_lane == wide_sub, rows, 0.0), axis=0, keepdims=True)

    def tree(values):
        while len(values) > 1:
            values = [a + b for a, b in zip(values[0::2], values[1::2])]
        return values[0]

    def to_member(index):
        return pltpu.make_async_remote_copy(
            src_ref=sum_ref,
            dst_ref=back_ref,
            send_sem=back_send.at[index],
            recv_sem=back_recv,
            device_id=member_at(index),
            device_id_type=MESH,
        )

    place = leader * members + member
    slot = (place // 8, pl.ds(lax.rem(place, 8), 1))

    def to_root(index):
        return pltpu.make_async_remote_copy(
            src_ref=mine_ref,
            dst_ref=all_sums.at[slot[0], slot[1]],
            send_sem=root_send.at[index],
            recv_sem=root_recv,
            device_id={"tor": index // columns, "pol": (index % columns) * GROUP + 1},
            device_id_type=MESH,
        )

    own = pltpu.make_async_copy(mine_ref, all_sums.at[slot[0], slot[1]], root_recv)
    order = sorted(range(roots), key=lambda r: r // columns + r % columns)

    def solve(total):
        row_lane = lax.broadcasted_iota(jnp.int32, (1, 128), 1)
        gram = [[None] * (ITERS + 1) for _ in range(ITERS + 1)]
        for index, (i, j) in enumerate(PAIRS):
            entry = jnp.sum(jnp.where(row_lane == index, total, 0.0), axis=1, keepdims=True)
            entry = jnp.broadcast_to(entry, (1, 128))
            gram[i][j] = entry
            gram[j][i] = entry
        alphas, estimates = small_solve(gram, gram[0][0])
        est = jnp.zeros((1, 128), F32)
        for index in range(ITERS):
            est = jnp.where(row_lane == index, estimates[index] * scale, est)
        for index in range(ITERS):
            weights_ref[index : index + 1, :] = alphas[index]
        weights_ref[ITERS : ITERS + 1, :] = est

    mine_ref[...] = mine

    @pl.when(jnp.logical_not(is_root))
    def _():
        for index in order:
            to_root(index).start()
        for copy in flying:
            copy.wait_send()
        for index in order:
            to_root(index).wait_send()
        to_member(0).wait_recv()
        solve(back_ref[...])

    @pl.when(is_root)
    def _():
        own.start()
        for index in order:

            @pl.when(root != index)
            def _():
                to_root(index).start()

        for copy in flying:
            copy.wait_send()
        for index in order:

            @pl.when(root != index)
            def _():
                to_root(index).wait_send()

        pltpu.make_async_copy(all_sums, all_sums, root_recv).wait()
        total = tree([all_sums[m] for m in range(tors * pols // 8)])
        total = jnp.sum(total, axis=0, keepdims=True)
        sum_ref[...] = total
        for_members(lambda index: to_member(index).start())
        solve(total)
        for_members(lambda index: to_member(index).wait_send())


def combine(t_ref, weights_ref, update_ref, est_ref):
    est_ref[...] = weights_ref[ITERS, 0:ITERS]
    full = []
    for k in range(ITERS):
        alpha = weights_ref[k : k + 1, :]
        full.append(jnp.broadcast_to(jnp.concatenate([alpha, alpha], axis=1), (8, 256)))
    for c in range(6):
        update_ref[c] = full[0] * t_ref[0, c] + full[1] * t_ref[1, c] + full[2] * t_ref[2, c]


def solution(mesh):
    sizes = (mesh.shape["tor"], mesh.shape["pol"])

    def shards(plasma_state, right_side, resistivity, jacobi_blocks):
        scale = 1.0 / float(plasma_state.size * sizes[0] * sizes[1]) ** 0.5
        hbm = pl.BlockSpec(memory_space=pl.ANY)
        vmem = pl.BlockSpec(memory_space=pltpu.VMEM)
        tangents, weights = pl.pallas_call(
            functools.partial(kernel, sizes, scale),
            out_shape=(pltpu.VMEM((ITERS, 6, 8, 256), F32), pltpu.VMEM((ITERS + 1, 128), F32)),
            in_specs=[hbm] * 4,
            out_specs=(vmem, vmem),
            scratch_shapes=[
                pltpu.VMEM((6, 8, 256), F32),
                pltpu.VMEM((6, 8, 256), F32),
                pltpu.VMEM((8, 256), F32),
                pltpu.VMEM((36, 8, 256), F32),
                pltpu.VMEM((ITERS + 1, 6, 8, 256), F32),
                pltpu.VMEM((6, 8, 256), F32),
                pltpu.VMEM((6, 8, 256), F32),
                pltpu.VMEM((4, 48, 256), BF16),
                pltpu.VMEM((4, 2, 48, 256), BF16),
                pltpu.VMEM((4, 2, 6, 256), F32),
                pltpu.VMEM((4, 2, 6, 256), F32),
                pltpu.VMEM((2, 64, 256), BF16),
                pltpu.VMEM((2, 64, 256), BF16),
                pltpu.VMEM((2, 8, 256), F32),
                pltpu.VMEM((2, 8, 256), F32),
                pltpu.VMEM((1, 128), F32),
                pltpu.VMEM((1, 128), F32),
                pltpu.VMEM((1, 128), F32),
                pltpu.VMEM((64, 8, 128), F32),
                pltpu.SemaphoreType.DMA((9,)),
                pltpu.SemaphoreType.DMA((4, 2)),
                pltpu.SemaphoreType.DMA((4, 2)),
                pltpu.SemaphoreType.DMA((4, 2)),
                pltpu.SemaphoreType.DMA((4, 2)),
                pltpu.SemaphoreType.DMA((33,)),
                pltpu.SemaphoreType.DMA,
                pltpu.SemaphoreType.DMA((16,)),
                pltpu.SemaphoreType.DMA,
            ],
            compiler_params=pltpu.CompilerParams(collective_id=0, has_side_effects=True),
            name="krylov",
        )(
            plasma_state.reshape(6, 8, 256),
            right_side.reshape(6, 8, 256),
            resistivity.reshape(8, 256),
            jacobi_blocks.reshape(36, 8, 256),
        )
        update, est = pl.pallas_call(
            combine,
            out_shape=(jax.ShapeDtypeStruct((6, 8, 256), F32), jax.ShapeDtypeStruct((ITERS,), F32)),
            in_specs=[vmem] * 2,
            out_specs=(vmem, vmem),
            name="combine",
        )(
            pltpu.with_memory_space_constraint(tangents, pltpu.VMEM),
            pltpu.with_memory_space_constraint(weights, pltpu.VMEM),
        )
        return update.reshape(6, 1, 8, 256), est

    return jax.shard_map(
        shards,
        mesh=mesh,
        in_specs=(
            P(None, "tor", "pol", None),
            P(None, "tor", "pol", None),
            P("tor", "pol", None),
            P(None, None, "tor", "pol", None),
        ),
        out_specs=(P(None, "tor", "pol", None), P()),
        check_vma=False,
    )
```

```python
import functools

import jax
import jax.numpy as jnp
from jax import lax
from jax.experimental import pallas as pl
from jax.experimental.pallas import tpu as pltpu
from jax.sharding import PartitionSpec as P

ITERS = 3
inverse_step = 1.0
viscosity = 0.2
epsilon = 1e-06

MESH = pl.DeviceIdType.MESH
F32 = jnp.float32
BF16 = jnp.bfloat16
PAIRS = [(i, j) for j in range(ITERS + 1) for i in range(j + 1)]
GROUP = 8


def flux(p, t, k):
    B, V, b, w = p[0:3], p[3:6], t[0:3], t[3:6]
    parts = []
    for i in range(3):
        parts.append(None if i == k else w[k] * B[i] + V[k] * b[i] - b[k] * V[i] - B[k] * w[i])
    for i in range(3):
        moment = w[k] * V[i] + V[k] * w[i] - b[k] * B[i] - B[k] * b[i]
        if i == k:
            moment = moment + (B[0] * b[0] + B[1] * b[1] + B[2] * b[2])
        parts.append(moment)
    return parts


def small_solve(gram, like):
    count = ITERS
    zero = jnp.zeros_like(like)
    norm0 = jnp.sqrt(gram[0][0] + epsilon)
    coefs = [[1.0 / norm0]]
    columns = []
    for j in range(count):
        shifted = [None] + coefs[j]
        size = j + 2
        applied = []
        for row in range(size):
            total = None
            for col in range(1, size):
                term = gram[row][col] * shifted[col]
                total = term if total is None else total + term
            applied.append(total)
        column = []
        for i in range(j + 1):
            total = None
            for row in range(i + 1):
                term = coefs[i][row] * applied[row]
                total = term if total is None else total + term
            column.append(total)
        remainder = []
        for row in range(size):
            total = shifted[row]
            for i in range(j + 1):
                if row <= i:
                    term = column[i] * coefs[i][row]
                    total = -term if total is None else total - term
            remainder.append(total)
        square = None
        for row in range(size):
            inner = None
            for col in range(size):
                term = gram[row][col] * remainder[col]
                inner = term if inner is None else inner + term
            term = inner * remainder[row]
            square = term if square is None else square + term
        norm = jnp.sqrt(jnp.maximum(square, 0.0) + epsilon)
        columns.append(column + [norm])
        if j + 1 < count:
            inverse = 1.0 / norm
            coefs.append([entry * inverse for entry in remainder])
    rhs = [norm0] + [zero] * count
    cosines, sines, triangle, estimates = [], [], [], []
    for column in range(count):
        entries = list(columns[column])
        for i in range(column):
            first, second = entries[i], entries[i + 1]
            entries[i] = cosines[i] * first + sines[i] * second
            entries[i + 1] = cosines[i] * second - sines[i] * first
        first, second = entries[column], entries[column + 1]
        radius = jnp.sqrt(first * first + second * second)
        inverse = 1.0 / radius
        cosine, sine = first * inverse, second * inverse
        cosines.append(cosine)
        sines.append(sine)
        triangle.append(entries[:column] + [inverse])
        previous = rhs[column]
        rhs[column] = cosine * previous
        rhs[column + 1] = -sine * previous
        estimates.append(jnp.abs(rhs[column + 1]))
    weights = [zero] * count
    for column in reversed(range(count)):
        value = rhs[column]
        for later in range(column + 1, count):
            value = value - triangle[later][column] * weights[later]
        weights[column] = value * triangle[column][column]
    alphas = []
    for row in range(count):
        total = None
        for j in range(row, count):
            term = weights[j] * coefs[j][row]
            total = term if total is None else total + term
        alphas.append(total)
    return alphas, estimates


def kernel(sizes, scale, plasma_hbm, right_hbm, resist_hbm, blocks_hbm, t_ref, weights_ref,
           plasma, right, resist, blocks, w_ref, up_ref, down_ref,
           tor_tx, tor_rx, pol_tx, pol_rx, mix_tx, mix_rx, edge_tx, edge_rx, mine_ref, back_ref, sum_ref, all_sums, size_ref,
           load_sem, tor_send, tor_recv, pol_send, pol_recv,
           root_send, root_recv, back_send, back_recv):
    tors, pols = sizes
    halves = 2
    width = tors // halves
    columns = pols // GROUP
    members = halves * GROUP
    leaders = width * columns
    tor = lax.axis_index("tor")
    pol = lax.axis_index("pol")
    tor_next, tor_prev = lax.rem(tor + 1, tors), lax.rem(tor + tors - 1, tors)
    pol_next, pol_prev = lax.rem(pol + 1, pols), lax.rem(pol + pols - 1, pols)

    half, lead_tor = tor // width, lax.rem(tor, width)
    column, inner = pol // GROUP, lax.rem(pol, GROUP)
    member = half * GROUP + inner
    leader = lead_tor * columns + column
    roots = leaders + 1
    root = tor * columns + column
    is_root = jnp.logical_and(inner == 1, root < roots)

    def member_at(index):
        return {"tor": (index // GROUP) * width + lead_tor, "pol": column * GROUP + index % GROUP}

    def root_at(index):
        return {"tor": index // columns, "pol": lax.rem(index, columns) * GROUP + 1}

    def for_members(act):
        @pl.when(root != 0)
        def _():
            for index in range(members):
                if index not in (1, GROUP + 1):
                    act(index)

        @pl.when(jnp.logical_and(root != 0, root != leaders))
        def _():
            act(GROUP + 1)


    barrier = pltpu.get_barrier_semaphore()
    for neighbour in (tor_next, tor_prev):
        pl.semaphore_signal(barrier, inc=1, device_id={"tor": neighbour, "pol": pol}, device_id_type=MESH)
    for neighbour in (pol_next, pol_prev):
        pl.semaphore_signal(barrier, inc=1, device_id={"tor": tor, "pol": neighbour}, device_id_type=MESH)

    loads = [
        pltpu.make_async_copy(plasma_hbm, plasma, load_sem.at[0]),
        pltpu.make_async_copy(right_hbm, right, load_sem.at[1]),
        pltpu.make_async_copy(resist_hbm, resist, load_sem.at[2]),
    ]
    loads.append(pltpu.make_async_copy(blocks_hbm, blocks, load_sem.at[3]))
    for load in loads:
        load.start()

    @pl.when(is_root)
    def _():
        for step in range(1, roots):
            partner = root_at(lax.rem(root + step, roots))
            pl.semaphore_signal(barrier, inc=1, device_id=partner, device_id_type=MESH)
        pl.semaphore_wait(barrier, 4 + roots - 1)
        for_members(
            lambda index: pl.semaphore_signal(barrier, inc=1, device_id=member_at(index), device_id_type=MESH)
        )

    lane = lax.broadcasted_iota(jnp.int32, (8, 256), 1)
    sub = lax.broadcasted_iota(jnp.int32, (8, 256), 0)

    def up_depth(x):
        return jnp.where(lane == 255, 0.0, pltpu.roll(x, 255, 1))

    def down_depth(x):
        return jnp.where(lane == 0, 0.0, pltpu.roll(x, 1, 1))

    def up_row(x, halo):
        return jnp.where(sub == 7, jnp.broadcast_to(halo, (8, 256)), pltpu.roll(x, 7, 0))

    def down_row(x, halo):
        return jnp.where(sub == 0, jnp.broadcast_to(halo, (8, 256)), pltpu.roll(x, 1, 0))

    def wait_bytes(ref, sem):
        pltpu.make_async_copy(ref, ref, sem).wait()

    def tor_copies(slot):
        return [
            pltpu.make_async_remote_copy(
                src_ref=tor_tx.at[slot],
                dst_ref=tor_rx.at[slot, way],
                send_sem=tor_send.at[0],
                recv_sem=tor_recv.at[slot],
                device_id={"tor": (tor_next, tor_prev)[way], "pol": pol},
                device_id_type=MESH,
            )
            for way in range(2)
        ]

    def pol_copies(slot):
        return [
            pltpu.make_async_remote_copy(
                src_ref=pol_tx.at[slot, way],
                dst_ref=pol_rx.at[slot, way],
                send_sem=pol_send.at[0],
                recv_sem=pol_recv.at[slot],
                device_id={"tor": tor, "pol": (pol_next, pol_prev)[way]},
                device_id_type=MESH,
            )
            for way in range(2)
        ]

    def mixed(t, direction):
        f = flux(own_plasma, t, direction)
        half = [None if f[c] is None else 0.5 * f[c] for c in range(6)]
        planes = []
        for sign in (-1.0, 1.0):
            planes.append(
                [sign * half[c] - viscosity * t[c] for c in (3, 4, 5)]
                + [t[0], t[1], t[2]]
                + [sign * half[c] for c in range(3) if c != direction]
            )
        return planes

    def mixed_copies(tor_way):
        if tor_way:
            src, dst, send, recv = mix_tx, mix_rx, tor_send, tor_recv
        else:
            src, dst, send, recv = edge_tx, edge_rx, pol_send, pol_recv
        return [
            pltpu.make_async_remote_copy(
                src_ref=src.at[way],
                dst_ref=dst.at[way],
                send_sem=send.at[1],
                recv_sem=recv.at[0],
                device_id=(
                    {"tor": (tor_next, tor_prev)[way], "pol": pol}
                    if tor_way
                    else {"tor": tor, "pol": (pol_next, pol_prev)[way]}
                ),
                device_id_type=MESH,
            )
            for way in range(2)
        ]

    def add_mixed(partial, planes, direction):
        partial = list(partial)
        others = [c for c in range(3) if c != direction]
        for index in range(3):
            partial[3 + index] = partial[3 + index] + planes[index]
            partial[index] = partial[index] - eta * planes[3 + index]
        for index, c in enumerate(others):
            partial[c] = partial[c] + planes[6 + index]
        return partial

    def pack_tor(slot, x):
        for pair in range(3):
            tor_tx[slot, 16 * pair : 16 * pair + 16, :] = jnp.concatenate(
                [x[2 * pair], x[2 * pair + 1]], axis=0
            ).astype(BF16)

    def pack_pol(slot, x):
        for c in range(6):
            pol_tx[slot, 0, c : c + 1, :] = x[c][7:8, :]
            pol_tx[slot, 1, c : c + 1, :] = x[c][0:1, :]

    def from_tor(slot, way):
        planes = []
        for pair in range(3):
            both = tor_rx[slot, way, 16 * pair : 16 * pair + 16, :].astype(F32)
            planes += [both[0:8], both[8:16]]
        return planes

    loads[0].wait()
    own_plasma = [plasma[c] for c in range(6)]
    pack_tor(3, own_plasma)
    pack_pol(3, own_plasma)
    loads[1].wait()
    for c in range(6):
        w_ref[0, c] = right[c]

    def precondition(k):
        vector = [w_ref[k, c] for c in range(6)]
        result = []
        for a in range(6):
            if k == 0 and a == 0:
                loads[3].wait()
            total = blocks[6 * a] * vector[0]
            for b in range(1, 6):
                total = total + blocks[6 * a + b] * vector[b]
            result.append(total)
        return result

    gram_rows = {}

    def product(i, j):
        total = None
        for c in range(6):
            term = w_ref[i, c] * w_ref[j, c]
            total = term if total is None else total + term
        total = total[:, 0:128] + total[:, 128:256]
        gram_rows[(i, j)] = jnp.sum(total, axis=0, keepdims=True)

    def local(t):
        f = flux(own_plasma, t, 2)
        partial = []
        for c in range(6):
            coefficient = eta if c < 3 else viscosity
            total = inverse_step * t[c] + coefficient * (6.0 * t[c] - up_depth(t[c]) - down_depth(t[c]))
            if f[c] is not None:
                half_flux = 0.5 * f[c]
                total = total + (up_depth(half_flux) - down_depth(half_flux))
            partial.append(total)
        return partial

    def outside(way, row):
        return jnp.where(pol == (pols - 1 if way == 1 else 0), 0.0, row)

    t = precondition(0)
    along_tor, along_pol = mixed(t, 0), mixed(t, 1)
    for way in range(2):
        for pair in range(4):
            mix_tx[way, 16 * pair : 16 * pair + 16, :] = jnp.concatenate(
                [along_tor[way][2 * pair], along_tor[way][2 * pair + 1]], axis=0
            ).astype(BF16)
        for index in range(8):
            edge_tx[way, index : index + 1, :] = along_pol[way][index][7 - 7 * way : 8 - 7 * way, :]

    @pl.when(jnp.logical_not(is_root))
    def _():
        pl.semaphore_wait(barrier, 4 + 1)

    tor_moves, pol_moves = mixed_copies(True), mixed_copies(False)
    state_moves = tor_copies(3) + pol_copies(3)
    for copy in tor_moves + pol_moves + state_moves:
        copy.start()
    for c in range(6):
        t_ref[0, c] = t[c]
    loads[2].wait()
    eta = resist[...]
    partial = local(t)
    product(0, 0)
    wait_bytes(edge_rx, pol_recv.at[0])
    after = [outside(1, edge_rx[1, index : index + 1, :]) for index in range(8)]
    before = [outside(0, edge_rx[0, index : index + 1, :]) for index in range(8)]
    partial = add_mixed(partial, [up_row(along_pol[1][index], after[index]) for index in range(8)], 1)
    partial = add_mixed(partial, [down_row(along_pol[0][index], before[index]) for index in range(8)], 1)
    wait_bytes(mix_rx, tor_recv.at[0])
    for way in range(2):
        planes = []
        for pair in range(4):
            both = mix_rx[way, 16 * pair : 16 * pair + 16, :].astype(F32)
            planes += [both[0:8], both[8:16]]
        partial = add_mixed(partial, planes, 0)
    for c in range(6):
        w_ref[1, c] = partial[c]

    for k in range(1, ITERS):
        t = precondition(k)
        pack_tor(k, t)
        tor_moves, pol_moves = tor_copies(k), pol_copies(k)
        for copy in tor_moves:
            copy.start()
        pack_pol(k, t)
        for copy in pol_moves:
            copy.start()
        for c in range(6):
            t_ref[k, c] = t[c]
        partial = local(t)
        for i in range(k + 1):
            product(i, k)
        if k == 1:
            wait_bytes(tor_rx.at[3], tor_recv.at[3])
            wait_bytes(pol_rx.at[3], pol_recv.at[3])
            for c in range(6):
                up_ref[c] = up_row(plasma[c], pol_rx[3, 1, c : c + 1, :])
                down_ref[c] = down_row(plasma[c], pol_rx[3, 0, c : c + 1, :])
        wait_bytes(pol_rx.at[k], pol_recv.at[k])
        t_up = [up_row(t[c], outside(1, pol_rx[k, 1, c : c + 1, :])) for c in range(6)]
        t_down = [down_row(t[c], outside(0, pol_rx[k, 0, c : c + 1, :])) for c in range(6)]
        f_up = flux([up_ref[c] for c in range(6)], t_up, 1)
        f_down = flux([down_ref[c] for c in range(6)], t_down, 1)
        for c in range(6):
            coefficient = eta if c < 3 else viscosity
            partial[c] = partial[c] - coefficient * (t_up[c] + t_down[c])
            if f_up[c] is not None:
                partial[c] = partial[c] + 0.5 * (f_up[c] - f_down[c])
        wait_bytes(tor_rx.at[k], tor_recv.at[k])
        t_up, t_down = from_tor(k, 1), from_tor(k, 0)
        f_up = flux(from_tor(3, 1), t_up, 0)
        f_down = flux(from_tor(3, 0), t_down, 0)
        for c in range(6):
            coefficient = eta if c < 3 else viscosity
            total = partial[c] - coefficient * (t_up[c] + t_down[c])
            if f_up[c] is not None:
                total = total + 0.5 * (f_up[c] - f_down[c])
            w_ref[k + 1, c] = total

    for i in range(ITERS + 1):
        product(i, ITERS)

    wide_lane = lax.broadcasted_iota(jnp.int32, (16, 128), 1)
    wide_sub = lax.broadcasted_iota(jnp.int32, (16, 128), 0)
    rows = jnp.zeros((16, 128), F32)
    for index, pair in enumerate(PAIRS):
        rows = jnp.where(wide_sub == index, jnp.broadcast_to(gram_rows[pair], (16, 128)), rows)
    rows = jnp.broadcast_to(jnp.sum(rows, axis=1, keepdims=True), (16, 128))
    mine = jnp.sum(jnp.where(wide_lane == wide_sub, rows, 0.0), axis=0, keepdims=True)

    def tree(values):
        while len(values) > 1:
            values = [a + b for a, b in zip(values[0::2], values[1::2])]
        return values[0]

    def to_member(index):
        return pltpu.make_async_remote_copy(
            src_ref=sum_ref,
            dst_ref=back_ref,
            send_sem=back_send,
            recv_sem=back_recv,
            device_id=member_at(index),
            device_id_type=MESH,
        )

    place = leader * members + member
    slot = (place // 8, pl.ds(lax.rem(place, 8), 1))

    def to_root(index):
        return pltpu.make_async_remote_copy(
            src_ref=mine_ref,
            dst_ref=all_sums.at[slot[0], slot[1]],
            send_sem=root_send,
            recv_sem=root_recv,
            device_id={"tor": index // columns, "pol": (index % columns) * GROUP + 1},
            device_id_type=MESH,
        )

    own = pltpu.make_async_copy(mine_ref, all_sums.at[slot[0], slot[1]], root_recv)
    order = sorted(range(roots), key=lambda r: r // columns + r % columns)

    def solve(total):
        row_lane = lax.broadcasted_iota(jnp.int32, (1, 128), 1)
        gram = [[None] * (ITERS + 1) for _ in range(ITERS + 1)]
        for index, (i, j) in enumerate(PAIRS):
            entry = jnp.sum(jnp.where(row_lane == index, total, 0.0), axis=1, keepdims=True)
            entry = jnp.broadcast_to(entry, (1, 128))
            gram[i][j] = entry
            gram[j][i] = entry
        alphas, estimates = small_solve(gram, gram[0][0])
        est = jnp.zeros((1, 128), F32)
        for index in range(ITERS):
            est = jnp.where(row_lane == index, estimates[index] * scale, est)
        for index in range(ITERS):
            weights_ref[index : index + 1, :] = alphas[index]
        weights_ref[ITERS : ITERS + 1, :] = est

    mine_ref[...] = mine

    def finish_halos():
        wait_bytes(tor_rx.at[pl.ds(1, ITERS)], tor_send.at[0])
        wait_bytes(mix_tx, tor_send.at[1])
        wait_bytes(pol_tx.at[pl.ds(1, ITERS)], pol_send.at[0])
        wait_bytes(edge_tx, pol_send.at[1])

    @pl.when(jnp.logical_not(is_root))
    def _():
        for index in order:
            to_root(index).start()
        finish_halos()
        wait_bytes(size_ref, root_send)
        to_member(0).wait_recv()
        solve(back_ref[...])

    @pl.when(is_root)
    def _():
        own.start()
        for index in order:

            @pl.when(root != index)
            def _():
                to_root(index).start()

        finish_halos()
        wait_bytes(size_ref.at[pl.ds(0, roots - 1)], root_send)
        pltpu.make_async_copy(all_sums, all_sums, root_recv).wait()
        total = tree([all_sums[m] for m in range(tors * pols // 8)])
        total = jnp.sum(total, axis=0, keepdims=True)
        sum_ref[...] = total
        for_members(lambda index: to_member(index).start())
        solve(total)

        @pl.when(jnp.logical_and(root != 0, root != leaders))
        def _():
            wait_bytes(size_ref.at[pl.ds(0, members - 1)], back_send)

        @pl.when(root == leaders)
        def _():
            wait_bytes(size_ref.at[pl.ds(0, members - 2)], back_send)


def combine(t_ref, weights_ref, update_ref, est_ref):
    est_ref[...] = weights_ref[ITERS, 0:ITERS]
    full = []
    for k in range(ITERS):
        alpha = weights_ref[k : k + 1, :]
        full.append(jnp.broadcast_to(jnp.concatenate([alpha, alpha], axis=1), (8, 256)))
    for c in range(6):
        update_ref[c] = full[0] * t_ref[0, c] + full[1] * t_ref[1, c] + full[2] * t_ref[2, c]


def solution(mesh):
    sizes = (mesh.shape["tor"], mesh.shape["pol"])

    def shards(plasma_state, right_side, resistivity, jacobi_blocks):
        scale = 1.0 / float(plasma_state.size * sizes[0] * sizes[1]) ** 0.5
        hbm = pl.BlockSpec(memory_space=pl.ANY)
        vmem = pl.BlockSpec(memory_space=pltpu.VMEM)
        tangents, weights = pl.pallas_call(
            functools.partial(kernel, sizes, scale),
            out_shape=(pltpu.VMEM((ITERS, 6, 8, 256), F32), pltpu.VMEM((ITERS + 1, 128), F32)),
            in_specs=[hbm] * 4,
            out_specs=(vmem, vmem),
            scratch_shapes=[
                pltpu.VMEM((6, 8, 256), F32),
                pltpu.VMEM((6, 8, 256), F32),
                pltpu.VMEM((8, 256), F32),
                pltpu.VMEM((36, 8, 256), F32),
                pltpu.VMEM((ITERS + 1, 6, 8, 256), F32),
                pltpu.VMEM((6, 8, 256), F32),
                pltpu.VMEM((6, 8, 256), F32),
                pltpu.VMEM((4, 48, 256), BF16),
                pltpu.VMEM((4, 2, 48, 256), BF16),
                pltpu.VMEM((4, 2, 6, 256), F32),
                pltpu.VMEM((4, 2, 6, 256), F32),
                pltpu.VMEM((2, 64, 256), BF16),
                pltpu.VMEM((2, 64, 256), BF16),
                pltpu.VMEM((2, 8, 256), F32),
                pltpu.VMEM((2, 8, 256), F32),
                pltpu.VMEM((1, 128), F32),
                pltpu.VMEM((1, 128), F32),
                pltpu.VMEM((1, 128), F32),
                pltpu.VMEM((64, 8, 128), F32),
                pltpu.VMEM((33, 1, 128), F32),
                pltpu.SemaphoreType.DMA((4,)),
                pltpu.SemaphoreType.DMA((2,)),
                pltpu.SemaphoreType.DMA((4,)),
                pltpu.SemaphoreType.DMA((2,)),
                pltpu.SemaphoreType.DMA((4,)),
                pltpu.SemaphoreType.DMA,
                pltpu.SemaphoreType.DMA,
                pltpu.SemaphoreType.DMA,
                pltpu.SemaphoreType.DMA,
            ],
            compiler_params=pltpu.CompilerParams(collective_id=0, has_side_effects=True),
            name="krylov",
        )(
            plasma_state.reshape(6, 8, 256),
            right_side.reshape(6, 8, 256),
            resistivity.reshape(8, 256),
            jacobi_blocks.reshape(36, 8, 256),
        )
        update, est = pl.pallas_call(
            combine,
            out_shape=(jax.ShapeDtypeStruct((6, 8, 256), F32), jax.ShapeDtypeStruct((ITERS,), F32)),
            in_specs=[vmem] * 2,
            out_specs=(vmem, vmem),
            name="combine",
        )(
            pltpu.with_memory_space_constraint(tangents, pltpu.VMEM),
            pltpu.with_memory_space_constraint(weights, pltpu.VMEM),
        )
        return update.reshape(6, 1, 8, 256), est

    return jax.shard_map(
        shards,
        mesh=mesh,
        in_specs=(
            P(None, "tor", "pol", None),
            P(None, "tor", "pol", None),
            P("tor", "pol", None),
            P(None, None, "tor", "pol", None),
        ),
        out_specs=(P(None, "tor", "pol", None), P()),
        check_vma=False,
    )
```

```python
import functools

import jax
import jax.numpy as jnp
from jax import lax
from jax.experimental import pallas as pl
from jax.experimental.pallas import tpu as pltpu
from jax.sharding import PartitionSpec as P

ITERS = 3
inverse_step = 1.0
viscosity = 0.2
epsilon = 1e-06

MESH = pl.DeviceIdType.MESH
F32 = jnp.float32
BF16 = jnp.bfloat16
PAIRS = [(i, j) for j in range(ITERS + 1) for i in range(j + 1)]
GROUP = 8


def flux(p, t, k):
    B, V, b, w = p[0:3], p[3:6], t[0:3], t[3:6]
    parts = []
    for i in range(3):
        parts.append(None if i == k else w[k] * B[i] + V[k] * b[i] - b[k] * V[i] - B[k] * w[i])
    for i in range(3):
        moment = w[k] * V[i] + V[k] * w[i] - b[k] * B[i] - B[k] * b[i]
        if i == k:
            moment = moment + (B[0] * b[0] + B[1] * b[1] + B[2] * b[2])
        parts.append(moment)
    return parts


def small_solve(gram, like):
    count = ITERS
    zero = jnp.zeros_like(like)
    norm0 = jnp.sqrt(gram[0][0] + epsilon)
    coefs = [[1.0 / norm0]]
    columns = []
    for j in range(count):
        shifted = [None] + coefs[j]
        size = j + 2
        applied = []
        for row in range(size):
            total = None
            for col in range(1, size):
                term = gram[row][col] * shifted[col]
                total = term if total is None else total + term
            applied.append(total)
        column = []
        for i in range(j + 1):
            total = None
            for row in range(i + 1):
                term = coefs[i][row] * applied[row]
                total = term if total is None else total + term
            column.append(total)
        remainder = []
        for row in range(size):
            total = shifted[row]
            for i in range(j + 1):
                if row <= i:
                    term = column[i] * coefs[i][row]
                    total = -term if total is None else total - term
            remainder.append(total)
        square = None
        for row in range(size):
            inner = None
            for col in range(size):
                term = gram[row][col] * remainder[col]
                inner = term if inner is None else inner + term
            term = inner * remainder[row]
            square = term if square is None else square + term
        norm = jnp.sqrt(jnp.maximum(square, 0.0) + epsilon)
        columns.append(column + [norm])
        if j + 1 < count:
            inverse = 1.0 / norm
            coefs.append([entry * inverse for entry in remainder])
    rhs = [norm0] + [zero] * count
    cosines, sines, triangle, estimates = [], [], [], []
    for column in range(count):
        entries = list(columns[column])
        for i in range(column):
            first, second = entries[i], entries[i + 1]
            entries[i] = cosines[i] * first + sines[i] * second
            entries[i + 1] = cosines[i] * second - sines[i] * first
        first, second = entries[column], entries[column + 1]
        radius = jnp.sqrt(first * first + second * second)
        inverse = 1.0 / radius
        cosine, sine = first * inverse, second * inverse
        cosines.append(cosine)
        sines.append(sine)
        triangle.append(entries[:column] + [inverse])
        previous = rhs[column]
        rhs[column] = cosine * previous
        rhs[column + 1] = -sine * previous
        estimates.append(jnp.abs(rhs[column + 1]))
    weights = [zero] * count
    for column in reversed(range(count)):
        value = rhs[column]
        for later in range(column + 1, count):
            value = value - triangle[later][column] * weights[later]
        weights[column] = value * triangle[column][column]
    alphas = []
    for row in range(count):
        total = None
        for j in range(row, count):
            term = weights[j] * coefs[j][row]
            total = term if total is None else total + term
        alphas.append(total)
    return alphas, estimates


def kernel(sizes, scale, plasma_hbm, right_hbm, resist_hbm, blocks_hbm, t_ref, weights_ref,
           plasma, right, resist, blocks, w_ref, up_ref, down_ref,
           tor_tx, tor_rx, pol_tx, pol_rx, mix_tx, mix_rx, edge_tx, edge_rx, mine_ref, back_ref, sum_ref, all_sums, size_ref,
           load_sem, tor_send, tor_recv, pol_send, pol_recv,
           root_send, root_recv, back_send, back_recv):
    tors, pols = sizes
    halves = 2
    width = tors // halves
    columns = pols // GROUP
    members = halves * GROUP
    leaders = width * columns
    tor = lax.axis_index("tor")
    pol = lax.axis_index("pol")
    tor_next, tor_prev = lax.rem(tor + 1, tors), lax.rem(tor + tors - 1, tors)
    pol_next, pol_prev = lax.rem(pol + 1, pols), lax.rem(pol + pols - 1, pols)

    half, lead_tor = tor // width, lax.rem(tor, width)
    column, inner = pol // GROUP, lax.rem(pol, GROUP)
    member = half * GROUP + inner
    leader = lead_tor * columns + column
    roots = leaders + 1
    root = tor * columns + column
    is_root = jnp.logical_and(inner == 1, root < roots)

    def member_at(index):
        return {"tor": (index // GROUP) * width + lead_tor, "pol": column * GROUP + index % GROUP}

    def root_at(index):
        return {"tor": index // columns, "pol": lax.rem(index, columns) * GROUP + 1}

    def for_members(act):
        @pl.when(root != 0)
        def _():
            for index in range(members):
                if index not in (1, GROUP + 1):
                    act(index)

        @pl.when(jnp.logical_and(root != 0, root != leaders))
        def _():
            act(GROUP + 1)


    barrier = pltpu.get_barrier_semaphore()
    for neighbour in (tor_next, tor_prev):
        pl.semaphore_signal(barrier, inc=1, device_id={"tor": neighbour, "pol": pol}, device_id_type=MESH)
    for neighbour in (pol_next, pol_prev):
        pl.semaphore_signal(barrier, inc=1, device_id={"tor": tor, "pol": neighbour}, device_id_type=MESH)

    loads = [
        pltpu.make_async_copy(plasma_hbm, plasma, load_sem.at[0]),
        pltpu.make_async_copy(right_hbm, right, load_sem.at[1]),
        pltpu.make_async_copy(resist_hbm, resist, load_sem.at[2]),
    ]
    loads.append(pltpu.make_async_copy(blocks_hbm, blocks, load_sem.at[3]))
    for load in loads:
        load.start()

    @pl.when(is_root)
    def _():
        for step in range(1, roots):
            partner = root_at(lax.rem(root + step, roots))
            pl.semaphore_signal(barrier, inc=1, device_id=partner, device_id_type=MESH)
        pl.semaphore_wait(barrier, 4 + roots - 1)
        for_members(
            lambda index: pl.semaphore_signal(barrier, inc=1, device_id=member_at(index), device_id_type=MESH)
        )

    lane = lax.broadcasted_iota(jnp.int32, (8, 256), 1)
    sub = lax.broadcasted_iota(jnp.int32, (8, 256), 0)

    def up_depth(x):
        return jnp.where(lane == 255, 0.0, pltpu.roll(x, 255, 1))

    def down_depth(x):
        return jnp.where(lane == 0, 0.0, pltpu.roll(x, 1, 1))

    def up_row(x, halo):
        return jnp.where(sub == 7, jnp.broadcast_to(halo, (8, 256)), pltpu.roll(x, 7, 0))

    def down_row(x, halo):
        return jnp.where(sub == 0, jnp.broadcast_to(halo, (8, 256)), pltpu.roll(x, 1, 0))

    def wait_bytes(ref, sem):
        pltpu.make_async_copy(ref, ref, sem).wait()

    def tor_copies(slot):
        return [
            pltpu.make_async_remote_copy(
                src_ref=tor_tx.at[slot],
                dst_ref=tor_rx.at[slot, way],
                send_sem=tor_send.at[0],
                recv_sem=tor_recv.at[slot],
                device_id={"tor": (tor_next, tor_prev)[way], "pol": pol},
                device_id_type=MESH,
            )
            for way in range(2)
        ]

    def pol_copies(slot):
        return [
            pltpu.make_async_remote_copy(
                src_ref=pol_tx.at[slot, way],
                dst_ref=pol_rx.at[slot, way],
                send_sem=pol_send.at[0],
                recv_sem=pol_recv.at[slot],
                device_id={"tor": tor, "pol": (pol_next, pol_prev)[way]},
                device_id_type=MESH,
            )
            for way in range(2)
        ]

    def mixed(t, direction):
        f = flux(own_plasma, t, direction)
        half = [None if f[c] is None else 0.5 * f[c] for c in range(6)]
        planes = []
        for sign in (-1.0, 1.0):
            planes.append(
                [sign * half[c] - viscosity * t[c] for c in (3, 4, 5)]
                + [t[0], t[1], t[2]]
                + [sign * half[c] for c in range(3) if c != direction]
            )
        return planes

    def mixed_copies(tor_way):
        if tor_way:
            src, dst, send, recv = mix_tx, mix_rx, tor_send, tor_recv
        else:
            src, dst, send, recv = edge_tx, edge_rx, pol_send, pol_recv
        return [
            pltpu.make_async_remote_copy(
                src_ref=src.at[way],
                dst_ref=dst.at[way],
                send_sem=send.at[1],
                recv_sem=recv.at[0],
                device_id=(
                    {"tor": (tor_next, tor_prev)[way], "pol": pol}
                    if tor_way
                    else {"tor": tor, "pol": (pol_next, pol_prev)[way]}
                ),
                device_id_type=MESH,
            )
            for way in range(2)
        ]

    def add_mixed(partial, planes, direction):
        partial = list(partial)
        others = [c for c in range(3) if c != direction]
        for index in range(3):
            partial[3 + index] = partial[3 + index] + planes[index]
            partial[index] = partial[index] - eta * planes[3 + index]
        for index, c in enumerate(others):
            partial[c] = partial[c] + planes[6 + index]
        return partial

    def pack_tor(slot, x):
        for pair in range(3):
            tor_tx[slot, 16 * pair : 16 * pair + 16, :] = jnp.concatenate(
                [x[2 * pair], x[2 * pair + 1]], axis=0
            ).astype(BF16)

    def pack_pol(slot, x):
        for c in range(6):
            pol_tx[slot, 0, c : c + 1, :] = x[c][7:8, :]
            pol_tx[slot, 1, c : c + 1, :] = x[c][0:1, :]

    def from_tor(slot, way):
        planes = []
        for pair in range(3):
            both = tor_rx[slot, way, 16 * pair : 16 * pair + 16, :].astype(F32)
            planes += [both[0:8], both[8:16]]
        return planes

    loads[0].wait()
    own_plasma = [plasma[c] for c in range(6)]
    pack_tor(3, own_plasma)
    pack_pol(3, own_plasma)
    loads[1].wait()
    for c in range(6):
        w_ref[0, c] = right[c]

    def precondition(k):
        vector = [w_ref[k, c] for c in range(6)]
        result = []
        for a in range(6):
            if k == 0 and a == 0:
                loads[3].wait()
            total = blocks[6 * a] * vector[0]
            for b in range(1, 6):
                total = total + blocks[6 * a + b] * vector[b]
            result.append(total)
        return result

    gram_rows = {}

    def product(i, j):
        total = None
        for c in range(6):
            term = w_ref[i, c] * w_ref[j, c]
            total = term if total is None else total + term
        gram_rows[(i, j)] = total[:, 0:128] + total[:, 128:256]

    narrow_lane = lax.broadcasted_iota(jnp.int32, (8, 128), 1)

    def side_by_side(pairs, start):
        for pair in pairs:
            lanes = jnp.broadcast_to(jnp.sum(gram_rows[pair], axis=1, keepdims=True), (8, 128))
            start = jnp.where(narrow_lane == PAIRS.index(pair), lanes, start)
        return start

    def local(t):
        f = flux(own_plasma, t, 2)
        partial = []
        for c in range(6):
            coefficient = eta if c < 3 else viscosity
            total = inverse_step * t[c] + coefficient * (6.0 * t[c] - up_depth(t[c]) - down_depth(t[c]))
            if f[c] is not None:
                half_flux = 0.5 * f[c]
                total = total + (up_depth(half_flux) - down_depth(half_flux))
            partial.append(total)
        return partial

    def outside(way, row):
        return jnp.where(pol == (pols - 1 if way == 1 else 0), 0.0, row)

    t = precondition(0)
    along_tor, along_pol = mixed(t, 0), mixed(t, 1)
    for way in range(2):
        for pair in range(4):
            mix_tx[way, 16 * pair : 16 * pair + 16, :] = jnp.concatenate(
                [along_tor[way][2 * pair], along_tor[way][2 * pair + 1]], axis=0
            ).astype(BF16)
        for index in range(8):
            edge_tx[way, index : index + 1, :] = along_pol[way][index][7 - 7 * way : 8 - 7 * way, :]

    @pl.when(jnp.logical_not(is_root))
    def _():
        pl.semaphore_wait(barrier, 4 + 1)

    tor_moves, pol_moves = mixed_copies(True), mixed_copies(False)
    state_moves = tor_copies(3) + pol_copies(3)
    for copy in tor_moves + pol_moves + state_moves:
        copy.start()
    for c in range(6):
        t_ref[0, c] = t[c]
    loads[2].wait()
    eta = resist[...]
    partial = local(t)
    product(0, 0)
    wait_bytes(edge_rx, pol_recv.at[0])
    after = [outside(1, edge_rx[1, index : index + 1, :]) for index in range(8)]
    before = [outside(0, edge_rx[0, index : index + 1, :]) for index in range(8)]
    partial = add_mixed(partial, [up_row(along_pol[1][index], after[index]) for index in range(8)], 1)
    partial = add_mixed(partial, [down_row(along_pol[0][index], before[index]) for index in range(8)], 1)
    wait_bytes(mix_rx, tor_recv.at[0])
    for way in range(2):
        planes = []
        for pair in range(4):
            both = mix_rx[way, 16 * pair : 16 * pair + 16, :].astype(F32)
            planes += [both[0:8], both[8:16]]
        partial = add_mixed(partial, planes, 0)
    for c in range(6):
        w_ref[1, c] = partial[c]

    for k in range(1, ITERS):
        t = precondition(k)
        pack_tor(k, t)
        tor_moves, pol_moves = tor_copies(k), pol_copies(k)
        for copy in tor_moves:
            copy.start()
        pack_pol(k, t)
        for copy in pol_moves:
            copy.start()
        for c in range(6):
            t_ref[k, c] = t[c]
        partial = local(t)
        for i in range(k + 1):
            product(i, k)
        if k == ITERS - 1:
            known = side_by_side([pair for pair in PAIRS if pair[1] < ITERS], jnp.zeros((8, 128), F32))
        if k == 1:
            wait_bytes(tor_rx.at[3], tor_recv.at[3])
            wait_bytes(pol_rx.at[3], pol_recv.at[3])
            for c in range(6):
                up_ref[c] = up_row(plasma[c], pol_rx[3, 1, c : c + 1, :])
                down_ref[c] = down_row(plasma[c], pol_rx[3, 0, c : c + 1, :])
        wait_bytes(pol_rx.at[k], pol_recv.at[k])
        t_up = [up_row(t[c], outside(1, pol_rx[k, 1, c : c + 1, :])) for c in range(6)]
        t_down = [down_row(t[c], outside(0, pol_rx[k, 0, c : c + 1, :])) for c in range(6)]
        f_up = flux([up_ref[c] for c in range(6)], t_up, 1)
        f_down = flux([down_ref[c] for c in range(6)], t_down, 1)
        for c in range(6):
            coefficient = eta if c < 3 else viscosity
            partial[c] = partial[c] - coefficient * (t_up[c] + t_down[c])
            if f_up[c] is not None:
                partial[c] = partial[c] + 0.5 * (f_up[c] - f_down[c])
        wait_bytes(tor_rx.at[k], tor_recv.at[k])
        t_up, t_down = from_tor(k, 1), from_tor(k, 0)
        f_up = flux(from_tor(3, 1), t_up, 0)
        f_down = flux(from_tor(3, 0), t_down, 0)
        for c in range(6):
            coefficient = eta if c < 3 else viscosity
            total = partial[c] - coefficient * (t_up[c] + t_down[c])
            if f_up[c] is not None:
                total = total + 0.5 * (f_up[c] - f_down[c])
            w_ref[k + 1, c] = total

    for i in range(ITERS + 1):
        product(i, ITERS)

    known = side_by_side([pair for pair in PAIRS if pair[1] == ITERS], known)
    mine = jnp.sum(known, axis=0, keepdims=True)

    def tree(values):
        while len(values) > 1:
            values = [a + b for a, b in zip(values[0::2], values[1::2])]
        return values[0]

    def to_member(index):
        return pltpu.make_async_remote_copy(
            src_ref=sum_ref,
            dst_ref=back_ref,
            send_sem=back_send,
            recv_sem=back_recv,
            device_id=member_at(index),
            device_id_type=MESH,
        )

    place = leader * members + member
    slot = (place // 8, pl.ds(lax.rem(place, 8), 1))

    def to_root(index):
        return pltpu.make_async_remote_copy(
            src_ref=mine_ref,
            dst_ref=all_sums.at[slot[0], slot[1]],
            send_sem=root_send,
            recv_sem=root_recv,
            device_id={"tor": index // columns, "pol": (index % columns) * GROUP + 1},
            device_id_type=MESH,
        )

    own = pltpu.make_async_copy(mine_ref, all_sums.at[slot[0], slot[1]], root_recv)
    order = sorted(range(roots), key=lambda r: r // columns + r % columns)

    def solve(total):
        row_lane = lax.broadcasted_iota(jnp.int32, (1, 128), 1)
        gram = [[None] * (ITERS + 1) for _ in range(ITERS + 1)]
        for index, (i, j) in enumerate(PAIRS):
            entry = jnp.sum(jnp.where(row_lane == index, total, 0.0), axis=1, keepdims=True)
            entry = jnp.broadcast_to(entry, (1, 128))
            gram[i][j] = entry
            gram[j][i] = entry
        alphas, estimates = small_solve(gram, gram[0][0])
        est = jnp.zeros((1, 128), F32)
        for index in range(ITERS):
            est = jnp.where(row_lane == index, estimates[index] * scale, est)
        for index in range(ITERS):
            weights_ref[index : index + 1, :] = alphas[index]
        weights_ref[ITERS : ITERS + 1, :] = est

    mine_ref[...] = mine

    def finish_halos():
        wait_bytes(tor_rx.at[pl.ds(1, ITERS)], tor_send.at[0])
        wait_bytes(mix_tx, tor_send.at[1])
        wait_bytes(pol_tx.at[pl.ds(1, ITERS)], pol_send.at[0])
        wait_bytes(edge_tx, pol_send.at[1])

    @pl.when(jnp.logical_not(is_root))
    def _():
        for index in order:
            to_root(index).start()
        finish_halos()
        wait_bytes(size_ref, root_send)
        to_member(0).wait_recv()
        solve(back_ref[...])

    @pl.when(is_root)
    def _():
        own.start()
        for index in order:

            @pl.when(root != index)
            def _():
                to_root(index).start()

        finish_halos()
        wait_bytes(size_ref.at[pl.ds(0, roots - 1)], root_send)
        pltpu.make_async_copy(all_sums, all_sums, root_recv).wait()
        total = tree([all_sums[m] for m in range(tors * pols // 8)])
        total = jnp.sum(total, axis=0, keepdims=True)
        sum_ref[...] = total
        for_members(lambda index: to_member(index).start())
        solve(total)

        @pl.when(jnp.logical_and(root != 0, root != leaders))
        def _():
            wait_bytes(size_ref.at[pl.ds(0, members - 1)], back_send)

        @pl.when(root == leaders)
        def _():
            wait_bytes(size_ref.at[pl.ds(0, members - 2)], back_send)


def combine(t_ref, weights_ref, update_ref, est_ref):
    est_ref[...] = weights_ref[ITERS, 0:ITERS]
    full = []
    for k in range(ITERS):
        alpha = weights_ref[k : k + 1, :]
        full.append(jnp.broadcast_to(jnp.concatenate([alpha, alpha], axis=1), (8, 256)))
    for c in range(6):
        update_ref[c] = full[0] * t_ref[0, c] + full[1] * t_ref[1, c] + full[2] * t_ref[2, c]


def solution(mesh):
    sizes = (mesh.shape["tor"], mesh.shape["pol"])

    def shards(plasma_state, right_side, resistivity, jacobi_blocks):
        scale = 1.0 / float(plasma_state.size * sizes[0] * sizes[1]) ** 0.5
        hbm = pl.BlockSpec(memory_space=pl.ANY)
        vmem = pl.BlockSpec(memory_space=pltpu.VMEM)
        tangents, weights = pl.pallas_call(
            functools.partial(kernel, sizes, scale),
            out_shape=(pltpu.VMEM((ITERS, 6, 8, 256), F32), pltpu.VMEM((ITERS + 1, 128), F32)),
            in_specs=[hbm] * 4,
            out_specs=(vmem, vmem),
            scratch_shapes=[
                pltpu.VMEM((6, 8, 256), F32),
                pltpu.VMEM((6, 8, 256), F32),
                pltpu.VMEM((8, 256), F32),
                pltpu.VMEM((36, 8, 256), F32),
                pltpu.VMEM((ITERS + 1, 6, 8, 256), F32),
                pltpu.VMEM((6, 8, 256), F32),
                pltpu.VMEM((6, 8, 256), F32),
                pltpu.VMEM((4, 48, 256), BF16),
                pltpu.VMEM((4, 2, 48, 256), BF16),
                pltpu.VMEM((4, 2, 6, 256), F32),
                pltpu.VMEM((4, 2, 6, 256), F32),
                pltpu.VMEM((2, 64, 256), BF16),
                pltpu.VMEM((2, 64, 256), BF16),
                pltpu.VMEM((2, 8, 256), F32),
                pltpu.VMEM((2, 8, 256), F32),
                pltpu.VMEM((1, 128), F32),
                pltpu.VMEM((1, 128), F32),
                pltpu.VMEM((1, 128), F32),
                pltpu.VMEM((64, 8, 128), F32),
                pltpu.VMEM((33, 1, 128), F32),
                pltpu.SemaphoreType.DMA((4,)),
                pltpu.SemaphoreType.DMA((2,)),
                pltpu.SemaphoreType.DMA((4,)),
                pltpu.SemaphoreType.DMA((2,)),
                pltpu.SemaphoreType.DMA((4,)),
                pltpu.SemaphoreType.DMA,
                pltpu.SemaphoreType.DMA,
                pltpu.SemaphoreType.DMA,
                pltpu.SemaphoreType.DMA,
            ],
            compiler_params=pltpu.CompilerParams(collective_id=0, has_side_effects=True),
            name="krylov",
        )(
            plasma_state.reshape(6, 8, 256),
            right_side.reshape(6, 8, 256),
            resistivity.reshape(8, 256),
            jacobi_blocks.reshape(36, 8, 256),
        )
        update, est = pl.pallas_call(
            combine,
            out_shape=(jax.ShapeDtypeStruct((6, 8, 256), F32), jax.ShapeDtypeStruct((ITERS,), F32)),
            in_specs=[vmem] * 2,
            out_specs=(vmem, vmem),
            name="combine",
        )(
            pltpu.with_memory_space_constraint(tangents, pltpu.VMEM),
            pltpu.with_memory_space_constraint(weights, pltpu.VMEM),
        )
        return update.reshape(6, 1, 8, 256), est

    return jax.shard_map(
        shards,
        mesh=mesh,
        in_specs=(
            P(None, "tor", "pol", None),
            P(None, "tor", "pol", None),
            P("tor", "pol", None),
            P(None, None, "tor", "pol", None),
        ),
        out_specs=(P(None, "tor", "pol", None), P()),
        check_vma=False,
    )
```

```python
import functools

import jax
import jax.numpy as jnp
from jax import lax
from jax.experimental import pallas as pl
from jax.experimental.pallas import tpu as pltpu
from jax.sharding import PartitionSpec as P

ITERS = 3
inverse_step = 1.0
viscosity = 0.2
epsilon = 1e-06

MESH = pl.DeviceIdType.MESH
F32 = jnp.float32
BF16 = jnp.bfloat16
PAIRS = [(i, j) for j in range(ITERS + 1) for i in range(j + 1)]
GROUP = 8


def flux(p, t, k):
    B, V, b, w = p[0:3], p[3:6], t[0:3], t[3:6]
    parts = []
    for i in range(3):
        parts.append(None if i == k else w[k] * B[i] + V[k] * b[i] - b[k] * V[i] - B[k] * w[i])
    for i in range(3):
        moment = w[k] * V[i] + V[k] * w[i] - b[k] * B[i] - B[k] * b[i]
        if i == k:
            moment = moment + (B[0] * b[0] + B[1] * b[1] + B[2] * b[2])
        parts.append(moment)
    return parts


def small_solve(gram, like):
    count = ITERS
    zero = jnp.zeros_like(like)
    norm0 = jnp.sqrt(gram[0][0] + epsilon)
    coefs = [[1.0 / norm0]]
    columns = []
    for j in range(count):
        shifted = [None] + coefs[j]
        size = j + 2
        applied = []
        for row in range(size):
            total = None
            for col in range(1, size):
                term = gram[row][col] * shifted[col]
                total = term if total is None else total + term
            applied.append(total)
        column = []
        for i in range(j + 1):
            total = None
            for row in range(i + 1):
                term = coefs[i][row] * applied[row]
                total = term if total is None else total + term
            column.append(total)
        remainder = []
        for row in range(size):
            total = shifted[row]
            for i in range(j + 1):
                if row <= i:
                    term = column[i] * coefs[i][row]
                    total = -term if total is None else total - term
            remainder.append(total)
        square = None
        for row in range(size):
            inner = None
            for col in range(size):
                term = gram[row][col] * remainder[col]
                inner = term if inner is None else inner + term
            term = inner * remainder[row]
            square = term if square is None else square + term
        norm = jnp.sqrt(jnp.maximum(square, 0.0) + epsilon)
        columns.append(column + [norm])
        if j + 1 < count:
            inverse = 1.0 / norm
            coefs.append([entry * inverse for entry in remainder])
    rhs = [norm0] + [zero] * count
    cosines, sines, triangle, estimates = [], [], [], []
    for column in range(count):
        entries = list(columns[column])
        for i in range(column):
            first, second = entries[i], entries[i + 1]
            entries[i] = cosines[i] * first + sines[i] * second
            entries[i + 1] = cosines[i] * second - sines[i] * first
        first, second = entries[column], entries[column + 1]
        radius = jnp.sqrt(first * first + second * second)
        inverse = 1.0 / radius
        cosine, sine = first * inverse, second * inverse
        cosines.append(cosine)
        sines.append(sine)
        triangle.append(entries[:column] + [inverse])
        previous = rhs[column]
        rhs[column] = cosine * previous
        rhs[column + 1] = -sine * previous
        estimates.append(jnp.abs(rhs[column + 1]))
    weights = [zero] * count
    for column in reversed(range(count)):
        value = rhs[column]
        for later in range(column + 1, count):
            value = value - triangle[later][column] * weights[later]
        weights[column] = value * triangle[column][column]
    alphas = []
    for row in range(count):
        total = None
        for j in range(row, count):
            term = weights[j] * coefs[j][row]
            total = term if total is None else total + term
        alphas.append(total)
    return alphas, estimates


def kernel(sizes, scale, plasma_hbm, right_hbm, resist_hbm, blocks_hbm, t_ref, weights_ref,
           inputs, w_ref, up_ref, down_ref,
           tor_tx, tor_rx, pol_tx, pol_rx, mix_tx, mix_rx, edge_tx, edge_rx, mine_ref, back_ref, sum_ref, all_sums, size_ref,
           load_sem, tor_send, tor_recv, pol_send, pol_recv,
           root_send, root_recv, back_send, back_recv):
    plasma, right, blocks = inputs.at[pl.ds(0, 6)], inputs.at[pl.ds(6, 6)], inputs.at[pl.ds(12, 36)]
    resist = inputs.at[48]
    tors, pols = sizes
    halves = 2
    width = tors // halves
    columns = pols // GROUP
    members = halves * GROUP
    leaders = width * columns
    tor = lax.axis_index("tor")
    pol = lax.axis_index("pol")
    tor_next, tor_prev = lax.rem(tor + 1, tors), lax.rem(tor + tors - 1, tors)
    pol_next, pol_prev = lax.rem(pol + 1, pols), lax.rem(pol + pols - 1, pols)

    half, lead_tor = tor // width, lax.rem(tor, width)
    column, inner = pol // GROUP, lax.rem(pol, GROUP)
    member = half * GROUP + inner
    leader = lead_tor * columns + column
    roots = leaders + 1
    root = tor * columns + column
    is_root = jnp.logical_and(inner == 1, root < roots)

    def member_at(index):
        return {"tor": (index // GROUP) * width + lead_tor, "pol": column * GROUP + index % GROUP}

    def root_at(index):
        return {"tor": index // columns, "pol": lax.rem(index, columns) * GROUP + 1}

    def for_members(act):
        @pl.when(root != 0)
        def _():
            for index in range(members):
                if index not in (1, GROUP + 1):
                    act(index)

        @pl.when(jnp.logical_and(root != 0, root != leaders))
        def _():
            act(GROUP + 1)


    barrier = pltpu.get_barrier_semaphore()
    for neighbour in (tor_next, tor_prev):
        pl.semaphore_signal(barrier, inc=1, device_id={"tor": neighbour, "pol": pol}, device_id_type=MESH)
    for neighbour in (pol_next, pol_prev):
        pl.semaphore_signal(barrier, inc=1, device_id={"tor": tor, "pol": neighbour}, device_id_type=MESH)

    loads = [
        pltpu.make_async_copy(plasma_hbm, plasma, load_sem),
        pltpu.make_async_copy(right_hbm, right, load_sem),
        pltpu.make_async_copy(resist_hbm, resist, load_sem),
    ]
    loads.append(pltpu.make_async_copy(blocks_hbm, blocks, load_sem))
    for load in loads:
        load.start()

    @pl.when(is_root)
    def _():
        for step in range(1, roots):
            partner = root_at(lax.rem(root + step, roots))
            pl.semaphore_signal(barrier, inc=1, device_id=partner, device_id_type=MESH)
        pl.semaphore_wait(barrier, 4 + roots - 1)
        for_members(
            lambda index: pl.semaphore_signal(barrier, inc=1, device_id=member_at(index), device_id_type=MESH)
        )

    lane = lax.broadcasted_iota(jnp.int32, (8, 256), 1)
    sub = lax.broadcasted_iota(jnp.int32, (8, 256), 0)

    def up_depth(x):
        return jnp.where(lane == 255, 0.0, pltpu.roll(x, 255, 1))

    def down_depth(x):
        return jnp.where(lane == 0, 0.0, pltpu.roll(x, 1, 1))

    def up_row(x, halo):
        return jnp.where(sub == 7, jnp.broadcast_to(halo, (8, 256)), pltpu.roll(x, 7, 0))

    def down_row(x, halo):
        return jnp.where(sub == 0, jnp.broadcast_to(halo, (8, 256)), pltpu.roll(x, 1, 0))

    def wait_bytes(ref, sem):
        pltpu.make_async_copy(ref, ref, sem).wait()

    def tor_copies(slot):
        return [
            pltpu.make_async_remote_copy(
                src_ref=tor_tx.at[slot],
                dst_ref=tor_rx.at[slot, way],
                send_sem=tor_send.at[0],
                recv_sem=tor_recv.at[slot],
                device_id={"tor": (tor_next, tor_prev)[way], "pol": pol},
                device_id_type=MESH,
            )
            for way in range(2)
        ]

    def pol_copies(slot):
        return [
            pltpu.make_async_remote_copy(
                src_ref=pol_tx.at[slot, way],
                dst_ref=pol_rx.at[slot, way],
                send_sem=pol_send.at[0],
                recv_sem=pol_recv.at[slot],
                device_id={"tor": tor, "pol": (pol_next, pol_prev)[way]},
                device_id_type=MESH,
            )
            for way in range(2)
        ]

    def mixed(t, direction):
        f = flux(own_plasma, t, direction)
        half = [None if f[c] is None else 0.5 * f[c] for c in range(6)]
        planes = []
        for sign in (-1.0, 1.0):
            planes.append(
                [sign * half[c] - viscosity * t[c] for c in (3, 4, 5)]
                + [t[0], t[1], t[2]]
                + [sign * half[c] for c in range(3) if c != direction]
            )
        return planes

    def mixed_copies(tor_way):
        if tor_way:
            src, dst, send, recv = mix_tx, mix_rx, tor_send, tor_recv
        else:
            src, dst, send, recv = edge_tx, edge_rx, pol_send, pol_recv
        return [
            pltpu.make_async_remote_copy(
                src_ref=src.at[way],
                dst_ref=dst.at[way],
                send_sem=send.at[1],
                recv_sem=recv.at[0],
                device_id=(
                    {"tor": (tor_next, tor_prev)[way], "pol": pol}
                    if tor_way
                    else {"tor": tor, "pol": (pol_next, pol_prev)[way]}
                ),
                device_id_type=MESH,
            )
            for way in range(2)
        ]

    def add_mixed(partial, planes, direction):
        partial = list(partial)
        others = [c for c in range(3) if c != direction]
        for index in range(3):
            partial[3 + index] = partial[3 + index] + planes[index]
            partial[index] = partial[index] - eta * planes[3 + index]
        for index, c in enumerate(others):
            partial[c] = partial[c] + planes[6 + index]
        return partial

    def pack_tor(slot, x):
        for pair in range(3):
            tor_tx[slot, 16 * pair : 16 * pair + 16, :] = jnp.concatenate(
                [x[2 * pair], x[2 * pair + 1]], axis=0
            ).astype(BF16)

    def pack_pol(slot, x):
        for c in range(6):
            pol_tx[slot, 0, c : c + 1, :] = x[c][7:8, :]
            pol_tx[slot, 1, c : c + 1, :] = x[c][0:1, :]

    def from_tor(slot, way):
        planes = []
        for pair in range(3):
            both = tor_rx[slot, way, 16 * pair : 16 * pair + 16, :].astype(F32)
            planes += [both[0:8], both[8:16]]
        return planes

    pltpu.make_async_copy(inputs, inputs, load_sem).wait()
    own_plasma = [plasma[c] for c in range(6)]
    pack_tor(3, own_plasma)
    pack_pol(3, own_plasma)
    for c in range(6):
        w_ref[0, c] = right[c]

    def precondition(k):
        vector = [w_ref[k, c] for c in range(6)]
        result = []
        for a in range(6):
            total = blocks[6 * a] * vector[0]
            for b in range(1, 6):
                total = total + blocks[6 * a + b] * vector[b]
            result.append(total)
        return result

    gram_rows = {}

    def product(i, j):
        total = None
        for c in range(6):
            term = w_ref[i, c] * w_ref[j, c]
            total = term if total is None else total + term
        total = total[:, 0:128] + total[:, 128:256]
        gram_rows[(i, j)] = jnp.sum(total, axis=0, keepdims=True)

    def local(t):
        f = flux(own_plasma, t, 2)
        partial = []
        for c in range(6):
            coefficient = eta if c < 3 else viscosity
            total = inverse_step * t[c] + coefficient * (6.0 * t[c] - up_depth(t[c]) - down_depth(t[c]))
            if f[c] is not None:
                half_flux = 0.5 * f[c]
                total = total + (up_depth(half_flux) - down_depth(half_flux))
            partial.append(total)
        return partial

    def outside(way, row):
        return jnp.where(pol == (pols - 1 if way == 1 else 0), 0.0, row)

    t = precondition(0)
    along_tor, along_pol = mixed(t, 0), mixed(t, 1)
    for way in range(2):
        for pair in range(4):
            mix_tx[way, 16 * pair : 16 * pair + 16, :] = jnp.concatenate(
                [along_tor[way][2 * pair], along_tor[way][2 * pair + 1]], axis=0
            ).astype(BF16)
        for index in range(8):
            edge_tx[way, index : index + 1, :] = along_pol[way][index][7 - 7 * way : 8 - 7 * way, :]

    @pl.when(jnp.logical_not(is_root))
    def _():
        pl.semaphore_wait(barrier, 4 + 1)

    tor_moves, pol_moves = mixed_copies(True), mixed_copies(False)
    state_moves = tor_copies(3) + pol_copies(3)
    for copy in tor_moves + pol_moves + state_moves:
        copy.start()
    for c in range(6):
        t_ref[0, c] = t[c]
    eta = resist[...]
    partial = local(t)
    product(0, 0)
    wait_bytes(edge_rx, pol_recv.at[0])
    after = [outside(1, edge_rx[1, index : index + 1, :]) for index in range(8)]
    before = [outside(0, edge_rx[0, index : index + 1, :]) for index in range(8)]
    partial = add_mixed(partial, [up_row(along_pol[1][index], after[index]) for index in range(8)], 1)
    partial = add_mixed(partial, [down_row(along_pol[0][index], before[index]) for index in range(8)], 1)
    wait_bytes(mix_rx, tor_recv.at[0])
    for way in range(2):
        planes = []
        for pair in range(4):
            both = mix_rx[way, 16 * pair : 16 * pair + 16, :].astype(F32)
            planes += [both[0:8], both[8:16]]
        partial = add_mixed(partial, planes, 0)
    for c in range(6):
        w_ref[1, c] = partial[c]

    for k in range(1, ITERS):
        t = precondition(k)
        pack_tor(k, t)
        tor_moves, pol_moves = tor_copies(k), pol_copies(k)
        for copy in tor_moves:
            copy.start()
        pack_pol(k, t)
        for copy in pol_moves:
            copy.start()
        for c in range(6):
            t_ref[k, c] = t[c]
        partial = local(t)
        for i in range(k + 1):
            product(i, k)
        if k == 1:
            wait_bytes(tor_rx.at[3], tor_recv.at[3])
            wait_bytes(pol_rx.at[3], pol_recv.at[3])
            for c in range(6):
                up_ref[c] = up_row(plasma[c], pol_rx[3, 1, c : c + 1, :])
                down_ref[c] = down_row(plasma[c], pol_rx[3, 0, c : c + 1, :])
        wait_bytes(pol_rx.at[k], pol_recv.at[k])
        t_up = [up_row(t[c], outside(1, pol_rx[k, 1, c : c + 1, :])) for c in range(6)]
        t_down = [down_row(t[c], outside(0, pol_rx[k, 0, c : c + 1, :])) for c in range(6)]
        f_up = flux([up_ref[c] for c in range(6)], t_up, 1)
        f_down = flux([down_ref[c] for c in range(6)], t_down, 1)
        for c in range(6):
            coefficient = eta if c < 3 else viscosity
            partial[c] = partial[c] - coefficient * (t_up[c] + t_down[c])
            if f_up[c] is not None:
                partial[c] = partial[c] + 0.5 * (f_up[c] - f_down[c])
        wait_bytes(tor_rx.at[k], tor_recv.at[k])
        t_up, t_down = from_tor(k, 1), from_tor(k, 0)
        f_up = flux(from_tor(3, 1), t_up, 0)
        f_down = flux(from_tor(3, 0), t_down, 0)
        for c in range(6):
            coefficient = eta if c < 3 else viscosity
            total = partial[c] - coefficient * (t_up[c] + t_down[c])
            if f_up[c] is not None:
                total = total + 0.5 * (f_up[c] - f_down[c])
            w_ref[k + 1, c] = total

    for i in range(ITERS + 1):
        product(i, ITERS)

    wide_lane = lax.broadcasted_iota(jnp.int32, (16, 128), 1)
    wide_sub = lax.broadcasted_iota(jnp.int32, (16, 128), 0)
    rows = jnp.zeros((16, 128), F32)
    for index, pair in enumerate(PAIRS):
        rows = jnp.where(wide_sub == index, jnp.broadcast_to(gram_rows[pair], (16, 128)), rows)
    rows = jnp.broadcast_to(jnp.sum(rows, axis=1, keepdims=True), (16, 128))
    mine = jnp.sum(jnp.where(wide_lane == wide_sub, rows, 0.0), axis=0, keepdims=True)

    def tree(values):
        while len(values) > 1:
            values = [a + b for a, b in zip(values[0::2], values[1::2])]
        return values[0]

    def to_member(index):
        return pltpu.make_async_remote_copy(
            src_ref=sum_ref,
            dst_ref=back_ref,
            send_sem=back_send,
            recv_sem=back_recv,
            device_id=member_at(index),
            device_id_type=MESH,
        )

    place = leader * members + member
    slot = (place // 8, pl.ds(lax.rem(place, 8), 1))

    def to_root(index):
        return pltpu.make_async_remote_copy(
            src_ref=mine_ref,
            dst_ref=all_sums.at[slot[0], slot[1]],
            send_sem=root_send,
            recv_sem=root_recv,
            device_id={"tor": index // columns, "pol": (index % columns) * GROUP + 1},
            device_id_type=MESH,
        )

    own = pltpu.make_async_copy(mine_ref, all_sums.at[slot[0], slot[1]], root_recv)
    order = sorted(range(roots), key=lambda r: r // columns + r % columns)

    def solve(total):
        row_lane = lax.broadcasted_iota(jnp.int32, (1, 128), 1)
        gram = [[None] * (ITERS + 1) for _ in range(ITERS + 1)]
        for index, (i, j) in enumerate(PAIRS):
            entry = jnp.sum(jnp.where(row_lane == index, total, 0.0), axis=1, keepdims=True)
            entry = jnp.broadcast_to(entry, (1, 128))
            gram[i][j] = entry
            gram[j][i] = entry
        alphas, estimates = small_solve(gram, gram[0][0])
        est = jnp.zeros((1, 128), F32)
        for index in range(ITERS):
            est = jnp.where(row_lane == index, estimates[index] * scale, est)
        for index in range(ITERS):
            weights_ref[index : index + 1, :] = alphas[index]
        weights_ref[ITERS : ITERS + 1, :] = est

    mine_ref[...] = mine

    def finish_halos():
        wait_bytes(tor_rx.at[pl.ds(1, ITERS)], tor_send.at[0])
        wait_bytes(mix_tx, tor_send.at[1])
        wait_bytes(pol_tx.at[pl.ds(1, ITERS)], pol_send.at[0])
        wait_bytes(edge_tx, pol_send.at[1])

    @pl.when(jnp.logical_not(is_root))
    def _():
        for index in order:
            to_root(index).start()
        finish_halos()
        wait_bytes(size_ref, root_send)
        to_member(0).wait_recv()
        solve(back_ref[...])

    @pl.when(is_root)
    def _():
        own.start()
        for index in order:

            @pl.when(root != index)
            def _():
                to_root(index).start()

        finish_halos()
        wait_bytes(size_ref.at[pl.ds(0, roots - 1)], root_send)
        pltpu.make_async_copy(all_sums, all_sums, root_recv).wait()
        total = tree([all_sums[m] for m in range(tors * pols // 8)])
        total = jnp.sum(total, axis=0, keepdims=True)
        sum_ref[...] = total
        for_members(lambda index: to_member(index).start())
        solve(total)

        @pl.when(jnp.logical_and(root != 0, root != leaders))
        def _():
            wait_bytes(size_ref.at[pl.ds(0, members - 1)], back_send)

        @pl.when(root == leaders)
        def _():
            wait_bytes(size_ref.at[pl.ds(0, members - 2)], back_send)


def combine(t_ref, weights_ref, update_ref, est_ref):
    est_ref[...] = weights_ref[ITERS, 0:ITERS]
    full = []
    for k in range(ITERS):
        alpha = weights_ref[k : k + 1, :]
        full.append(jnp.broadcast_to(jnp.concatenate([alpha, alpha], axis=1), (8, 256)))
    for c in range(6):
        update_ref[c] = full[0] * t_ref[0, c] + full[1] * t_ref[1, c] + full[2] * t_ref[2, c]


def solution(mesh):
    sizes = (mesh.shape["tor"], mesh.shape["pol"])

    def shards(plasma_state, right_side, resistivity, jacobi_blocks):
        scale = 1.0 / float(plasma_state.size * sizes[0] * sizes[1]) ** 0.5
        hbm = pl.BlockSpec(memory_space=pl.ANY)
        vmem = pl.BlockSpec(memory_space=pltpu.VMEM)
        tangents, weights = pl.pallas_call(
            functools.partial(kernel, sizes, scale),
            out_shape=(pltpu.VMEM((ITERS, 6, 8, 256), F32), pltpu.VMEM((ITERS + 1, 128), F32)),
            in_specs=[hbm] * 4,
            out_specs=(vmem, vmem),
            scratch_shapes=[
                pltpu.VMEM((49, 8, 256), F32),
                pltpu.VMEM((ITERS + 1, 6, 8, 256), F32),
                pltpu.VMEM((6, 8, 256), F32),
                pltpu.VMEM((6, 8, 256), F32),
                pltpu.VMEM((4, 48, 256), BF16),
                pltpu.VMEM((4, 2, 48, 256), BF16),
                pltpu.VMEM((4, 2, 6, 256), F32),
                pltpu.VMEM((4, 2, 6, 256), F32),
                pltpu.VMEM((2, 64, 256), BF16),
                pltpu.VMEM((2, 64, 256), BF16),
                pltpu.VMEM((2, 8, 256), F32),
                pltpu.VMEM((2, 8, 256), F32),
                pltpu.VMEM((1, 128), F32),
                pltpu.VMEM((1, 128), F32),
                pltpu.VMEM((1, 128), F32),
                pltpu.VMEM((64, 8, 128), F32),
                pltpu.VMEM((33, 1, 128), F32),
                pltpu.SemaphoreType.DMA,
                pltpu.SemaphoreType.DMA((2,)),
                pltpu.SemaphoreType.DMA((4,)),
                pltpu.SemaphoreType.DMA((2,)),
                pltpu.SemaphoreType.DMA((4,)),
                pltpu.SemaphoreType.DMA,
                pltpu.SemaphoreType.DMA,
                pltpu.SemaphoreType.DMA,
                pltpu.SemaphoreType.DMA,
            ],
            compiler_params=pltpu.CompilerParams(collective_id=0, has_side_effects=True),
            name="krylov",
        )(
            plasma_state.reshape(6, 8, 256),
            right_side.reshape(6, 8, 256),
            resistivity.reshape(8, 256),
            jacobi_blocks.reshape(36, 8, 256),
        )
        update, est = pl.pallas_call(
            combine,
            out_shape=(jax.ShapeDtypeStruct((6, 8, 256), F32), jax.ShapeDtypeStruct((ITERS,), F32)),
            in_specs=[vmem] * 2,
            out_specs=(vmem, vmem),
            name="combine",
        )(
            pltpu.with_memory_space_constraint(tangents, pltpu.VMEM),
            pltpu.with_memory_space_constraint(weights, pltpu.VMEM),
        )
        return update.reshape(6, 1, 8, 256), est

    return jax.shard_map(
        shards,
        mesh=mesh,
        in_specs=(
            P(None, "tor", "pol", None),
            P(None, "tor", "pol", None),
            P("tor", "pol", None),
            P(None, None, "tor", "pol", None),
        ),
        out_specs=(P(None, "tor", "pol", None), P()),
        check_vma=False,
    )
```
